32 devices in a mesh: wide: 8 (over z, y), narrow: 4 (over x, core).
Axes of the slice: x: 2, y: 2, z: 4, core: 2. Of those that a mesh axis runs over, the one named last changes fastest.
Arguments:
- right_side: float32 [112, 224, 256], P('narrow', 'wide'), may hold values from -60 to 60
- initial_guess: float32 [112, 224, 256], P('narrow', 'wide'), may hold values from -6 to 6
- class_map: int32 [112, 224], P('narrow', 'wide'), may hold values from 0 to 7
- class_conductivity: float32 [8], replicated, may hold values from 0.2 to 2
- window_index: int32 [4, 8, 1024], P('narrow', 'wide'), may hold values from 0 to 1023, each once within a row
- local_inverse: float32 [4, 8, 1024, 1024], P('narrow', 'wide'), may hold values from -1 to 1
- coarse_basis: float32 [4, 8, 4, 1024], P('narrow', 'wide'), may hold values from -0.1875 to 0.1875
- coarse_inverse: float32 [128, 128], P('wide', 'narrow'), may hold values from -8 to 8
Outputs:
- solution: float32 [112, 224, 256], P('narrow', 'wide')
- residual: float32 [112, 224, 256], P('narrow', 'wide')
The draws below stay inside these ranges and needn't reach their ends.
All inputs are finite; a program needn't handle non-finite values.
Results may differ from the reference program's by a relative error of at most 0.00013.
Values sent between devices are 32-bit elements; how exact they have to be, the bound alone decides.
A program may use at most 64 MiB of HBM per device.

```python
import math
import jax
import jax.numpy as jnp
from jax import lax

ES = 32
OV = 2
MODES = 4
ITERS = 3
CLASSES = 8
NRHS = 256
CS = 28
LOCAL = 1024
SROWS = 4
SCOLS = 8
NX = 112
NY = 224
NC = 128


def draw_right_side(key, part):
    key_noise = jax.random.fold_in(key, 11)
    col_pos = jnp.arange(NY, dtype=jnp.float32)[None, :, None]
    across = jnp.exp(math.log(10.0) * col_pos / (NY - 1))
    sample = jax.random.truncated_normal(key_noise, -6.0, 6.0, (NX, NY, NRHS), jnp.float32)
    return sample * across


def draw_local_inverse(key, part):
    key_off = jax.random.fold_in(key, 23)
    shape_full = (SROWS, SCOLS, LOCAL, LOCAL)
    identity = jnp.eye(LOCAL, dtype=jnp.float32)
    sample = jax.random.truncated_normal(key_off, -6.0, 6.0, shape_full, jnp.float32)
    return 0.25 * (identity + sample * (0.6 / math.sqrt(LOCAL)))


def draw_coarse_inverse(key, part):
    key_off = jax.random.fold_in(key, 31)
    rows_all = jnp.arange(NC, dtype=jnp.int32)
    mode_of = rows_all % MODES
    srow_of = rows_all // MODES % SROWS
    scol_of = rows_all // (MODES * SROWS)
    paired = (srow_of * SCOLS + scol_of) * MODES + mode_of
    identity = (paired[:, None] == rows_all[None, :]).astype(jnp.float32)
    sample = jax.random.truncated_normal(key_off, -6.0, 6.0, (NC, NC), jnp.float32)
    return 4.0 * identity + sample * (2.0 / math.sqrt(NC))


def set_ends(array, key, low, high):
    index_at = [jax.random.randint(jax.random.fold_in(key, axis), (), 0, length) for axis, length in enumerate(array.shape)]
    widest = array.shape.index(max(array.shape))
    neighbour = index_at[:widest] + [(index_at[widest] + 1) % array.shape[widest]] + index_at[widest + 1:]
    return array.at[tuple(index_at)].set(low).at[tuple(neighbour)].set(high)


def block_scale(stream_key, shape, cuts, least, high):
    factor_of = 1.0
    for position, parts in cuts:
        heights = jax.random.uniform(jax.random.fold_in(jax.random.fold_in(stream_key, 6), position), (parts,), jnp.float32, least / len(cuts), high / len(cuts))
        factor_of = factor_of * jnp.repeat(jnp.exp(heights), shape[position] // parts).reshape((-1,) + (1,) * (len(shape) - 1 - position))
    return factor_of


def normal_values(stream_key, dims, scale, reach, shards=(), kind=jnp.bfloat16):
    drawn = scale * jax.random.normal(stream_key, dims, jnp.float32)
    if shards:
        drawn = drawn * block_scale(stream_key, dims, shards, -0.22, 0.18)
    return jnp.clip(drawn, -reach, reach).astype(kind)


def setup_inputs(seed: int = 0) -> dict:
    streams_of = jax.random.split(jax.random.key(seed), 9)
    right_side = draw_right_side(jax.random.fold_in(streams_of[8], 71), 0)
    initial_guess = normal_values(streams_of[1], (NX, NY, NRHS), 1.0, 6.0, ((0, 4), (1, 8)), jnp.float32)
    class_map = set_ends(jax.random.randint(streams_of[2], (NX, NY), 0, CLASSES), jax.random.fold_in(streams_of[2], 1), 0, CLASSES - 1).astype(jnp.int32)
    class_conductivity = jnp.clip(jnp.exp(jax.random.uniform(streams_of[3], (CLASSES,), jnp.float32, math.log(0.2), math.log(2.0))), 0.2, 2.0)
    window_index = jax.vmap(lambda own: jax.random.permutation(own, LOCAL))(jax.random.split(streams_of[4], SROWS * SCOLS)).reshape((SROWS, SCOLS, LOCAL)).astype(jnp.int32)
    local_inverse = draw_local_inverse(jax.random.fold_in(streams_of[8], 71), 0)
    coarse_basis = normal_values(streams_of[6], (SROWS, SCOLS, MODES, LOCAL), LOCAL ** -0.5, 0.1875, ((0, 4), (1, 8)), jnp.float32)
    coarse_inverse = draw_coarse_inverse(jax.random.fold_in(streams_of[8], 71), 0)
    return dict(right_side=right_side, initial_guess=initial_guess, class_map=class_map, class_conductivity=class_conductivity, window_index=window_index, local_inverse=local_inverse, coarse_basis=coarse_basis, coarse_inverse=coarse_inverse)


HIGHEST = lax.Precision.HIGHEST
REACTION = 0.01
NEIGHBOURS = ((0, 1), (2, 1), (1, 0), (1, 2))


def apply_operator(padded_field, conduct):
    height = padded_field.shape[0] - 2
    breadth = padded_field.shape[1] - 2
    centre = padded_field[1:height + 1, 1:breadth + 1]
    own_conduct = conduct[1:height + 1, 1:breadth + 1]
    result = REACTION * centre
    for row_shift, col_shift in NEIGHBOURS:
        beside = padded_field[row_shift:row_shift + height, col_shift:col_shift + breadth]
        face_weight = 0.5 * (own_conduct + conduct[row_shift:row_shift + height, col_shift:col_shift + breadth])
        result = result + face_weight[:, :, None] * (centre - beside)
    return result


def reference(right_side, initial_guess, class_map, class_conductivity, window_index, local_inverse, coarse_basis, coarse_inverse):
    conduct = class_conductivity[class_map]
    conduct_pad = jnp.pad(conduct, 1)

    def operate(values):
        return apply_operator(jnp.pad(values, ((1, 1), (1, 1), (0, 0))), conduct_pad)

    row_index = jnp.arange(SROWS, dtype=jnp.int32)[:, None] * CS + jnp.arange(ES, dtype=jnp.int32)[None, :]
    col_index = jnp.arange(SCOLS, dtype=jnp.int32)[:, None] * CS + jnp.arange(ES, dtype=jnp.int32)[None, :]
    inverse_order = jnp.argsort(window_index, axis=-1).astype(jnp.int32)
    solution = initial_guess
    residual = right_side - operate(solution)
    for iteration in range(ITERS):
        padded_res = jnp.pad(residual, ((OV, OV), (OV, OV), (0, 0)))
        windows = padded_res[row_index[:, None, :, None], col_index[None, :, None, :]]
        windows = windows.reshape(SROWS, SCOLS, ES * ES, NRHS)
        gathered = jnp.take_along_axis(windows, window_index[:, :, :, None], axis=2)
        local_part = jnp.einsum("abkl,ablr->abkr", local_inverse, gathered, precision=HIGHEST)
        coarse_rhs = jnp.einsum("abmk,abkr->abmr", coarse_basis, gathered, precision=HIGHEST).reshape(NC, NRHS)
        coarse_sol = jnp.dot(coarse_inverse, coarse_rhs, precision=HIGHEST, preferred_element_type=jnp.float32)
        coarse_sol = coarse_sol.reshape(SCOLS, SROWS, MODES, NRHS).transpose(1, 0, 2, 3)
        extended = local_part + jnp.einsum("abmk,abmr->abkr", coarse_basis, coarse_sol, precision=HIGHEST)
        windowed = jnp.take_along_axis(extended, inverse_order[:, :, :, None], axis=2)
        windowed = windowed.reshape(SROWS, SCOLS, ES, ES, NRHS)
        direction = windowed[:, :, OV:OV + CS, OV:OV + CS].transpose(0, 2, 1, 3, 4).reshape(NX, NY, NRHS)
        image = operate(direction)
        stepsize = jnp.sum(residual * image, axis=(0, 1)) / jnp.sum(image * image, axis=(0, 1))
        solution = solution + stepsize * direction
        residual = residual - stepsize * image
    return solution, residual
```

```python
import functools
import math
import types

import jax
import jax.numpy as jnp
from jax import lax
from jax.experimental import pallas as pl
from jax.experimental.pallas import tpu as pltpu
from jax.sharding import PartitionSpec as P

ITERS = 3
REACTION = 0.01
LANES = 128
SUB = 8
F32 = jnp.float32
BF16 = jnp.bfloat16
MESH = pl.DeviceIdType.MESH
DIRS = ((-1, -1), (-1, 0), (-1, 1), (0, -1), (0, 1), (1, -1), (1, 0), (1, 1))

SIDES = (3, 4, 0, 2, 5, 7)
ENDS = (1, 6)


def split(value):
    high = value.astype(BF16)
    return high, (value - high.astype(F32)).astype(BF16)


def dot(left, right):
    return jnp.dot(left, right, preferred_element_type=F32)


def dot3(left_high, left_low, right_high, right_low):
    return dot(left_high, right_high) + (dot(left_low, right_high) + dot(left_high, right_low))


def half(h):
    return slice(h * LANES, (h + 1) * LANES)


def kernel(cfg, names, *refs):
    N, W, ES, OV, CS, COLS, MODES, KR = cfg
    rhs_ref, guess_ref, map_ref, class_ref, wrow_ref, inv_hbm, basis_ref, coarse_ref = refs[:8]
    sol_out, res_out = refs[8:10]
    s = types.SimpleNamespace(**dict(zip(names, refs[10:])))
    H = OV + 1
    lo, hi = OV, OV + CS - H
    LOCAL = ES * ES
    DW = ES + 2
    RP = s.daux.shape[0]
    HV = COLS // LANES
    LK = 3 * MODES * N
    HALF = N // 2
    CHIPS = HALF * W
    base = hi - (ES - SUB)
    a = lax.axis_index("narrow")
    b = lax.axis_index("wide")
    core = lax.rem(a, 2)
    me = (a // 2) * W + b

    def at(u, t):
        return (u + 1) * DW + t + 1

    def other(k):
        idx = lax.rem(me + k, CHIPS)
        return idx, (lax.rem(idx, W), 2 * (idx // W) + core)

    def valid(d):
        da, db = DIRS[d]
        return (a + da >= 0) & (a + da < N) & (b + db >= 0) & (b + db < W)

    barrier = pltpu.get_barrier_semaphore()

    def greet(k, carry):
        pl.semaphore_signal(barrier, inc=1, device_id=other(k)[1], device_id_type=MESH)
        return carry

    lax.fori_loop(1, CHIPS, greet, 0)
    count = CHIPS - 1
    for d, (da, db) in enumerate(DIRS):
        if da != 0:
            ok = valid(d)
            count = count + ok.astype(jnp.int32)

            @pl.when(ok)
            def _():
                pl.semaphore_signal(barrier, inc=1, device_id=(b + db, a + da), device_id_type=MESH)

    load = pltpu.make_async_copy(inv_hbm, s.inv, s.lsem)
    load.start()

    def landing(d, rows, cols, corners, away):
        da, db = DIRS[d]
        if away:
            da, db = -da, -db
        if db == 0:
            return rows((da + 1) // 2)
        if da == 0:
            return cols((db + 1) // 2)
        return corners((da + 1) + (db + 1) // 2)

    groups = [
        (s.g_row, s.g_col, None),
        (s.c_row, s.c_col, s.c_cor),
        (s.a_row, s.a_col, s.a_cor),
        (s.r_row, s.r_col, s.r_cor),
    ]
    groups += [(s.z_row.at[i], s.z_col.at[i], s.z_cor.at[i]) for i in range(ITERS)]

    for d in range(8):

        @pl.when(jnp.logical_not(valid(d)))
        def _():
            for rows, cols, corners in groups:
                if corners is None and 0 not in DIRS[d]:
                    continue
                pick = lambda ref: lambda i: ref.at[i]
                ref = landing(d, pick(rows), pick(cols), corners is not None and pick(corners), False)
                ref[...] = jnp.zeros(ref.shape, F32)

    def exchange(slot, rows, cols, corners):
        copies = {}
        for d in range(8):
            if corners is None and 0 not in DIRS[d]:
                continue
            da, db = DIRS[d]
            to = groups[slot]
            pick = lambda ref: lambda i: ref.at[i]
            copies[d] = pltpu.make_async_remote_copy(
                src_ref=landing(d, rows, cols, corners, False),
                dst_ref=landing(d, pick(to[0]), pick(to[1]), to[2] is not None and pick(to[2]), True),
                send_sem=s.ssem.at[slot, d],
                recv_sem=s.rsem.at[slot, 7 - d],
                device_id=(b + db, a + da),
                device_id_type=MESH,
            )
        return copies

    def send(copies, dirs=SIDES + ENDS):
        for d in dirs:
            if d in copies:

                @pl.when(valid(d))
                def _():
                    copies[d].start()

    def recv(copies):
        for d in copies:

            @pl.when(valid(d))
            def _():
                copies[7 - d].wait_recv()

    def done(copies):
        for d in copies:

            @pl.when(valid(d))
            def _():
                copies[d].wait_send()

    def gather_copy(slot, k, ref, rows):
        _, target = other(k)
        part = ref.at[a, b, rows]
        return pltpu.make_async_remote_copy(
            src_ref=part,
            dst_ref=part,
            send_sem=s.gs.at[slot, k],
            recv_sem=s.gr.at[slot, me],
            device_id=target,
            device_id_type=MESH,
        )

    def forward(slot, k, ref, rows, mine):
        idx, _ = other(k)
        row = 2 * (idx // W)
        part = ref.at[row + core, lax.rem(idx, W), rows]
        away = part if mine else ref.at[row + 1 - core, lax.rem(idx, W), rows]
        return pltpu.make_async_remote_copy(
            src_ref=part,
            dst_ref=away,
            send_sem=s.fs.at[slot, k],
            recv_sem=s.fr.at[slot, idx],
            device_id=(b, a + 1 - 2 * core),
            device_id_type=MESH,
        )

    def gather_send(slot, ref, rows):
        def body(k, carry):
            gather_copy(slot, k, ref, rows).start()
            return carry

        lax.fori_loop(1, CHIPS, body, 0)
        forward(slot, 0, ref, rows, True).start()

    def gather_recv(slot, ref, rows):
        def relay(k, carry):
            idx, target = other(k)
            pltpu.make_async_remote_copy(
                src_ref=ref.at[a, b, rows],
                dst_ref=ref.at[target[1], target[0], rows],
                send_sem=s.gs.at[slot, k],
                recv_sem=s.gr.at[slot, idx],
                device_id=target,
                device_id_type=MESH,
            ).wait_recv()
            forward(slot, k, ref, rows, True).start()
            return carry

        lax.fori_loop(1, CHIPS, relay, 0)

        def collect(k, carry):
            forward(slot, k, ref, rows, False).wait_recv()
            return carry

        lax.fori_loop(0, CHIPS, collect, 0)

    def gather_done(slot, ref, rows):
        def body(k, carry):
            gather_copy(slot, k, ref, rows).wait_send()
            return carry

        lax.fori_loop(1, CHIPS, body, 0)

        def sent(k, carry):
            forward(slot, k, ref, rows, True).wait_send()
            return carry

        lax.fori_loop(0, CHIPS, sent, 0)

    def edges_of_guess(i, carry):
        s.gs_col[0, pl.ds(i, 1), :] = guess_ref[i, 0:1, :]
        s.gs_col[1, pl.ds(i, 1), :] = guess_ref[i, CS - 1 : CS, :]
        return carry

    lax.fori_loop(0, CS, edges_of_guess, 0)
    classes = map_ref[...]
    conduct = jnp.zeros(classes.shape, F32)
    for k in range(class_ref.shape[0]):
        conduct = jnp.where(classes == k, class_ref[k], conduct)
    s.field[...] = jnp.zeros(s.field.shape, F32)
    s.field[0:CS, 0:CS] = conduct
    s.cfield[...] = jnp.transpose(s.field[...])[0:ES]
    run = MODES * W
    for i in range(MODES * N):
        line, left = divmod(i * run, COLS)
        s.k0[a, b, line : line + 1, left : left + run] = coarse_ref[i : i + 1]

    guess_sends = exchange(
        0, lambda i: guess_ref.at[i * (CS - 1)], lambda i: s.gs_col.at[i], None
    )
    tile = lambda i: s.cfield.at[pl.ds(i * (ES - SUB), SUB)]
    cond_sends = exchange(1, lambda i: s.cfield, tile, lambda i: tile(i % 2))
    pl.semaphore_wait(barrier, count)
    send(cond_sends)
    send(guess_sends)
    k_rows = pl.ds(0, KR)
    gather_send(0, s.k0, k_rows)

    step = 256
    numbering = wrow_ref[...]
    tall_numbering = jnp.transpose(jnp.broadcast_to(numbering, (LANES, LOCAL)))
    lane = lax.broadcasted_iota(jnp.int32, (LOCAL, LANES), 1)
    for c in range(0, LOCAL, LANES):
        s.perm_t[:, c : c + LANES] = jnp.where(lane + c == tall_numbering, 1.0, 0.0).astype(BF16)

    def hot(i, carry):
        off = pl.multiple_of(i * step, step)
        pos = lax.broadcasted_iota(jnp.int32, (step, LOCAL), 0) + off
        s.perm[pl.ds(off, step), :] = jnp.where(pos == numbering, 1.0, 0.0).astype(BF16)
        return carry

    lax.fori_loop(0, LOCAL // step, hot, 0)
    basis = basis_ref[0, 0]
    place = lax.rem(b, 3) * (MODES * N) + a * MODES
    line = lax.broadcasted_iota(jnp.int32, (LANES, LOCAL), 0) - place
    s.spread[...] = jnp.zeros(s.spread.shape, F32)
    for m in range(MODES):
        s.spread[...] = jnp.where(line == m, basis[m : m + 1], s.spread[...])
    b_high, b_low = split(jnp.transpose(s.spread[...]))
    s.aux[...] = dot(s.perm[...], b_high) + dot(s.perm[...], b_low)
    for k, first in enumerate((lo, hi)):
        for j in range(H):
            s.as_col[k, j] = s.aux[pl.ds(first + j, ES, stride=ES), :]
    aux_sends = exchange(
        2,
        lambda i: s.aux.at[pl.ds((lo, hi)[i] * ES, H * ES)],
        lambda i: s.as_col.at[i],
        lambda i: s.as_col.at[i % 2, pl.ds(0, H), pl.ds((ES - SUB) * (i // 2), SUB)],
    )

    def place_guess(i, carry):
        for h in range(HV):
            s.gd[h, pl.ds(at(OV + i, OV), CS), :] = guess_ref[i, :, half(h)]
            s.sol[h, i, 0:CS, :] = guess_ref[i, :, half(h)]
        return carry

    lax.fori_loop(0, CS, place_guess, 0)
    recv(guess_sends)
    recv(cond_sends)
    for h in range(HV):
        for side in range(2):
            edge = OV - 1 + side * (CS + 1)
            s.gd[h, pl.ds(at(edge, OV), CS), :] = s.g_row[side, :, half(h)]
            s.gd[h, pl.ds(at(OV, edge), CS, stride=DW), :] = s.g_col[side, :, half(h)]
    stack = (
        (s.c_cor.at[0], s.c_row.at[0], s.c_cor.at[1]),
        (s.c_col.at[0], s.cfield, s.c_col.at[1]),
        (s.c_cor.at[2], s.c_row.at[1], s.c_cor.at[3]),
    )
    for k, (left, mid, right) in enumerate(stack):
        s.cst[k, 0:H] = left[CS - H - (ES - SUB) : CS - (ES - SUB)]
        s.cst[k, H : H + CS] = mid[0:CS]
        s.cst[k, H + CS : DW] = right[0:H]
    clane = lax.broadcasted_iota(jnp.int32, s.cst.shape[1:], 1)
    cmap = jnp.where(
        clane < H,
        pltpu.roll(s.cst[0], LANES - (CS - H), 1),
        jnp.where(
            clane < H + CS, pltpu.roll(s.cst[1], H, 1), pltpu.roll(s.cst[2], H + CS, 1)
        ),
    )
    for r in range(DW):
        s.cond[pl.ds(r * DW, DW), :] = jnp.broadcast_to(cmap[0:DW, r : r + 1], (DW, LANES))
    col_pos = b * CS - OV + lax.broadcasted_iota(jnp.int32, (ES, LANES), 0)
    col_in = jnp.where((col_pos >= 0) & (col_pos < CS * W), 1.0, 0.0)

    def faces(u, carry):
        row_pos = a * CS - OV + u
        inside = jnp.where((row_pos >= 0) & (row_pos < CS * N), col_in, 0.0)
        cond = lambda du, dt: s.cond[pl.ds(at(u + du, dt), ES), :]
        own = cond(0, 0)
        halved = 0.5 * inside
        parts = [halved * (own + cond(*o)) for o in ((-1, 0), (1, 0), (0, -1), (0, 1))]
        here = pl.ds(pl.multiple_of(u * ES, ES), ES)
        s.wt[0, here, :] = REACTION * inside + ((parts[0] + parts[1]) + (parts[2] + parts[3]))
        for k in range(4):
            s.wt[1 + k, here, :] = parts[k]
        return carry

    lax.fori_loop(0, ES, faces, 0)

    def operator(read, u, t, n):
        weights = [s.wt[k, pl.ds(u * ES + t, n), :] for k in range(5)]
        out = []
        for h in range(HV):
            v = lambda du, dt: read(h, pl.ds(at(u + du, t + dt), n))
            around = weights[1] * v(-1, 0) + weights[2] * v(1, 0)
            beside = weights[3] * v(0, -1) + weights[4] * v(0, 1)
            out.append(weights[0] * v(0, 0) - (around + beside))
        return out

    def own_residual(i, carry):
        u = OV + i
        image = operator(lambda h, rows: s.gd[h, rows, :], u, OV, CS)
        for h in range(HV):
            s.res[h, pl.ds(u * ES + OV, CS), :] = rhs_ref[i, :, half(h)] - image[h]
        return carry

    lax.fori_loop(0, CS, own_residual, 0)

    near = (OV, CS)
    for k in range(2):
        for h in range(HV):
            for q in range(OV):
                s.rs_col[k, h, q] = s.res[h, pl.ds(near[k] + q, ES, stride=ES), :]
            s.rs_row[k, h] = s.res[h, near[k] * ES : (near[k] + OV) * ES, :]
    for k in range(4):
        for h in range(HV):
            for r in range(OV):
                cell = (near[k // 2] + r) * ES + near[k % 2]
                s.rs_cor[k, h, r * OV : (r + 1) * OV, :] = s.res[h, cell : cell + OV, :]
    res_sends = exchange(
        3,
        lambda i: s.rs_row.at[i],
        lambda i: s.rs_col.at[i],
        lambda i: s.rs_cor.at[i],
    )
    send(res_sends)
    send(aux_sends)

    load.wait()

    def right_side_perm(i, carry):
        rows = pl.ds(pl.multiple_of(i * step, step), step)
        high, low = split(s.inv[rows, :])
        s.t_high[rows, :] = dot(high, s.perm_t[...]).astype(BF16)
        s.t_low[rows, :] = dot(low, s.perm_t[...]).astype(BF16)
        return carry

    lax.fori_loop(0, LOCAL // step, right_side_perm, 0)
    line = lax.broadcasted_iota(jnp.int32, (2 * H * ES, LOCAL), 0)
    col = line >> int(math.log2(ES))
    col = jnp.where(col < H, col + lo, col - H + hi)
    pos = (line & (ES - 1)) * ES + col
    edge = jnp.where(pos == numbering, 1.0, 0.0).astype(BF16)
    s.e_high[...] = dot(edge, s.t_high[...]).astype(BF16)
    s.e_low[...] = dot(edge, s.t_low[...]).astype(BF16)
    m_high, m_low = split(jnp.concatenate([basis, jnp.zeros((SUB - MODES, LOCAL), F32)], axis=0))
    s.bw[...] = dot(jnp.concatenate([m_high, m_low], axis=0), s.perm_t[...]).astype(BF16)

    def set_x(u, value):
        high, low = split(jnp.concatenate(value, axis=1))
        rows = pl.ds(pl.multiple_of(u * ES, ES), ES)
        s.x_high[rows, :] = high
        s.x_low[rows, :] = low

    recv(res_sends)
    far = (0, OV + CS)
    for h in range(HV):
        for k in range(2):
            for q in range(OV):
                line = slice(q * ES + OV, q * ES + OV + CS)
                s.res[h, pl.ds((far[k] + q) * ES + OV, CS), :] = s.r_row[k, h, line, :]
                line = pl.ds(OV * ES + far[k] + q, CS, stride=ES)
                s.res[h, line, :] = s.r_col[k, h, q, OV : OV + CS, :]
        for k in range(4):
            for r in range(OV):
                cell = (far[k // 2] + r) * ES + far[k % 2]
                s.res[h, cell : cell + OV, :] = s.r_cor[k, h, r * OV : (r + 1) * OV, :]

    def first_x(u, carry):
        set_x(u, [s.res[h, pl.ds(u * ES, ES), :] for h in range(HV)])
        return carry

    lax.fori_loop(0, ES, first_x, 0)

    def coarse_rows():
        both = dot(s.bw[...], s.x_high[...])
        return both[0:SUB] + (both[SUB:] + dot(s.bw[0:SUB, :], s.x_low[...]))

    def left_side_perm(i, carry):
        rows = pl.ds(pl.multiple_of(i * step, step), step)
        s.l_high[rows, :] = dot(s.perm[rows, :], s.t_high[...]).astype(BF16)
        s.l_low[rows, :] = dot(s.perm[rows, :], s.t_low[...]).astype(BF16)
        return carry

    def build_phi():
        recv(aux_sends)
        for i in range(CS):
            s.daux[pl.ds(at(OV + i, OV), CS), :] = s.aux[pl.ds((OV + i) * ES + OV, CS), :]
        for k in range(2):
            for j in range(H):
                deep_line = k * (CS + H) + j
                s.daux[pl.ds(deep_line * DW + H, CS), :] = s.a_row[
                    k, j * ES + OV : j * ES + OV + CS, :
                ]
                s.daux[pl.ds(H * DW + deep_line, CS, stride=DW), :] = s.a_col[
                    k, j, OV : OV + CS, :
                ]
        for k in range(4):
            first = lo if k // 2 else base
            for q in range(H):
                cell = (k // 2) * (CS + H) * DW + (k % 2) * (CS + H) + q
                for r in range(H):
                    s.daux[pl.ds(cell + r * DW, 1), :] = s.a_cor[k, q, first + r : first + r + 1, :]
        chunk = RP // 2

        def body(i, carry):
            rows = pl.ds(pl.multiple_of(i * chunk, chunk), chunk)
            value = s.daux[rows, :]
            high = value.astype(BF16).astype(F32)
            low = value - high
            if 2 * LK <= LANES:
                s.phi[rows, 0:LANES] = (high + pltpu.roll(low, LK, 1)).astype(BF16)
                s.phi[rows, LANES:] = high.astype(BF16)
            else:
                s.phi[rows, 0:LANES] = high.astype(BF16)
                s.phi[rows, LANES : 2 * LANES] = low.astype(BF16)
                s.phi[rows, 2 * LANES :] = high.astype(BF16)
            return carry

        lax.fori_loop(0, 2, body, 0)

    def build_kmat():
        gather_recv(0, s.k0, k_rows)
        per = COLS // (4 * W)
        wide_cols = MODES * W
        group = MODES * N
        piece = lax.broadcasted_iota(jnp.int32, (group, COLS), 0) & (per - 1)
        lane = lax.broadcasted_iota(jnp.int32, (group, COLS), 1)
        keep = (lane >> int(math.log2(wide_cols))) == piece
        width = N * W * SUB
        j = lax.broadcasted_iota(jnp.int32, (COLS, width), 0) & (wide_cols - 1)
        c = lax.broadcasted_iota(jnp.int32, (COLS, width), 1)
        total_high = total_low = None
        for a2 in range(N):
            blocks = []
            for third in range(3):
                db = lax.rem(third - b + 1 + 3 * W, 3) - 1
                spot = jnp.clip(b + db, 0, W - 1)
                raw = s.k0[a2, spot, 0:KR, :]
                tall = jnp.concatenate(
                    [jnp.broadcast_to(raw[r : r + 1], (per, COLS)) for r in range(KR)], axis=0
                )
                blocks.append(jnp.where(keep, tall, 0.0))
            if 2 * LK <= LANES:
                blocks = blocks * 2
            fill = LANES - len(blocks) * group
            blocks.append(jnp.zeros((fill, COLS), F32))
            high, low = split(jnp.concatenate(blocks, axis=0))
            fold = c == a2 * (W * SUB) + (j >> 2) * SUB + (j & 3)
            fold = jnp.where(fold, 1.0, 0.0).astype(BF16)
            th, tl = dot(high, fold), dot(low, fold)
            total_high = th if total_high is None else total_high + th
            total_low = tl if total_low is None else total_low + tl
        s.kmat[0] = total_high.astype(BF16)
        s.kmat[1] = total_low.astype(BF16)

    sub_pos = lax.broadcasted_iota(jnp.int32, (SUB, COLS), 0)
    pending = [guess_sends, cond_sends, aux_sends, res_sends]
    numer = denom = None
    sizes = []
    spans = []
    for it in range(ITERS + 1):
        ref = s.g.at[it]
        first = MODES if it == ITERS else 0
        last = MODES if it == 0 else MODES + 2
        span = pl.ds(first, last - first)
        spans.append(span)
        rows = coarse_rows() if it < ITERS else jnp.zeros((SUB, COLS), F32)
        if it > 0:
            rows = jnp.where(sub_pos == MODES, numer, rows)
            rows = jnp.where(sub_pos == MODES + 1, denom, rows)
        ref[a, b] = rows
        gather_send(it + 1, ref, span)
        if it < ITERS:
            value = dot3(s.e_high[...], s.e_low[...], s.x_high[...], s.x_low[...])
            for k in range(2):
                for j in range(H):
                    line = (k * H + j) * ES
                    for h in range(HV):
                        s.zs_col[it, k, h, j] = value[line : line + ES, half(h)]
            for k in range(4):
                u0 = hi if k // 2 else lo
                skip = ((H - 1) * (k // 2), (H - 1) * (k % 2))
                n = 0
                for r in range(H):
                    for j in range(H):
                        if (r, j) == ((H - 1) - skip[0], (H - 1) - skip[1]):
                            continue
                        for h in range(HV):
                            s.zs_cor[it, k, h, n : n + 1, :] = s.zs_col[
                                it, k % 2, h, j, u0 + r : u0 + r + 1, :
                            ]
                        n += 1
            copies = exchange(
                4 + it,
                lambda i: s.zs_row.at[it, i],
                lambda i: s.zs_col.at[it, i],
                lambda i: s.zs_cor.at[it, i],
            )
            send(copies, SIDES)
            if it == 0:
                lax.fori_loop(0, LOCAL // step, left_side_perm, 0)

            def solve(i, carry):
                rows = pl.ds(pl.multiple_of(i * step, step), step)
                value = dot3(s.l_high[rows, :], s.l_low[rows, :], s.x_high[...], s.x_low[...])
                for j in range(step // ES):
                    u = i * (step // ES) + j
                    for h in range(HV):
                        s.wdeep[h, pl.ds(at(u, 0), ES), :] = value[j * ES : (j + 1) * ES, half(h)]
                return carry

            lax.fori_loop(0, LOCAL // step, solve, 0)
            for k, u in enumerate((lo, hi)):
                for h in range(HV):
                    for r in range(H):
                        s.zs_row[it, k, h, r] = s.wdeep[h, pl.ds(at(u + r, 0), ES), :]
            send(copies, ENDS)
            pending.append(copies)
        if it == 0:
            build_phi()
            build_kmat()
        if it >= 2:
            old = sizes[it - 2]

            def advance(i, carry):
                for h in range(HV):
                    here = s.deep[it % 2, h, pl.ds(at(OV + i, OV), CS), :]
                    s.sol[h, i, 0:CS, :] = s.sol[h, i, 0:CS, :] + old[:, half(h)] * here
                return carry

            lax.fori_loop(0, CS, advance, 0)
        gather_recv(it + 1, ref, span)
        everyone = ref[...].reshape(N * W, SUB, COLS)
        if it > 0:
            total = jnp.sum(everyone, axis=0)
            size = total[MODES : MODES + 1] / total[MODES + 1 : MODES + 2]
            sizes.append(size)
        if it == ITERS:
            break
        coarse_only = lax.broadcasted_iota(jnp.int32, everyone.shape, 1) < MODES
        everyone = jnp.where(coarse_only, everyone, 0.0)
        g_high, g_low = split(everyone.reshape(N * W * SUB, COLS))
        s_high, s_low = split(dot3(s.kmat[0], s.kmat[1], g_high, g_low))
        if 2 * LK <= LANES:
            s_all = jnp.concatenate([s_high, s_low], axis=0)
        else:
            s_all = jnp.concatenate([s_high, s_high, s_low], axis=0)
        recv(copies)
        for h in range(HV):
            for k in range(2):
                for j in range(H):
                    deep_line = k * (CS + H) + j
                    s.wdeep[h, pl.ds(deep_line * DW + H, CS), :] = s.z_row[
                        it, k, h, j, OV : OV + CS, :
                    ]
                    s.wdeep[h, pl.ds(H * DW + deep_line, CS, stride=DW), :] = s.z_col[
                        it, k, h, j, OV : OV + CS, :
                    ]
            for k in range(4):
                skip = ((H - 1) * (k // 2), (H - 1) * (k % 2))
                n = 0
                for r in range(H):
                    for j in range(H):
                        if (r, j) == skip:
                            continue
                        cell = ((k // 2) * (CS + H) + r) * DW + (k % 2) * (CS + H) + j
                        s.wdeep[h, pl.ds(cell, 1), :] = s.z_cor[it, k, h, n : n + 1, :]
                        n += 1
        chunk = RP // 2
        now, before = it % 2, 1 - it % 2

        def coarse_part(i, carry):
            rows = pl.ds(pl.multiple_of(i * chunk, chunk), chunk)
            value = dot(s.phi[rows, :], s_all)
            for h in range(HV):
                part = value[:, half(h)] + s.wdeep[h, rows, :]
                if it > 0:
                    part = s.deep[before, h, rows, :] - size[:, half(h)] * part
                s.deep[now, h, rows, :] = part
            return carry

        lax.fori_loop(0, 2, coarse_part, 0)
        read = lambda h, rows: s.deep[now, h, rows, :]
        if it < ITERS - 1:

            def margin(q, carry):
                u = jnp.where(q < OV, q, q + CS)
                set_x(u, operator(read, u, 0, ES))
                return carry

            lax.fori_loop(0, 2 * OV, margin, 0)

        def apply(i, carry):
            u = OV + i
            value = operator(read, u, 0, ES)
            if it < ITERS - 1:
                set_x(u, value)
            line = pl.ds(pl.multiple_of(u * ES, ES), ES)
            sums = []
            for h in range(HV):
                left = s.res[h, line, :]
                if it > 0:
                    left = left - size[:, half(h)] * s.img[h, i]
                    s.res[h, line, :] = left
                s.img[h, i] = value[h]
                sums.append(carry[2 * h] + left * value[h])
                sums.append(carry[2 * h + 1] + value[h] * value[h])
            return tuple(sums)

        nothing = jnp.zeros((ES, LANES), F32)
        sums = lax.fori_loop(0, CS, apply, (nothing,) * (2 * HV))
        col = lax.broadcasted_iota(jnp.int32, (ES, LANES), 0)
        mine = (col >= OV) & (col < OV + CS)
        sums = [jnp.sum(jnp.where(mine, v, 0.0), axis=0, keepdims=True) for v in sums]
        numer = jnp.concatenate(sums[0::2], axis=1)
        denom = jnp.concatenate(sums[1::2], axis=1)

    size = sizes[-1]

    def finish(i, carry):
        u = OV + i
        for h in range(HV):
            step_of = size[:, half(h)]
            here = s.deep[(ITERS - 1) % 2, h, pl.ds(at(u, OV), CS), :]
            sol_out[i, :, half(h)] = s.sol[h, i, 0:CS, :] + step_of * here
            here = s.img[h, i, OV : OV + CS, :]
            res_out[i, :, half(h)] = s.res[h, pl.ds(u * ES + OV, CS), :] - step_of * here
        return carry

    lax.fori_loop(0, CS, finish, 0)
    for copies in pending:
        done(copies)
    gather_done(0, s.k0, k_rows)
    for it in range(ITERS + 1):
        gather_done(it + 1, s.g.at[it], spans[it])


def local(
    N,
    W,
    right_side,
    initial_guess,
    class_map,
    class_conductivity,
    window_index,
    local_inverse,
    coarse_basis,
    coarse_inverse,
):
    CS, _, COLS = right_side.shape
    MODES, LOCAL = coarse_basis.shape[2:]
    ES = math.isqrt(LOCAL)
    OV = (ES - CS) // 2
    H = OV + 1
    DW = ES + 2
    RP = -(-DW * DW // 32) * 32
    HV = COLS // LANES
    KR = coarse_inverse.size // COLS
    K0 = -(-KR // SUB) * SUB
    CHIPS = N * W // 2
    PK = (2 if 6 * MODES * N <= LANES else 3) * LANES
    TALL = -(-DW // SUB) * SUB
    vmem = pl.BlockSpec(memory_space=pltpu.VMEM)
    scratch = dict(
        inv=((LOCAL, LOCAL), F32),
        perm=((LOCAL, LOCAL), BF16),
        perm_t=((LOCAL, LOCAL), BF16),
        t_high=((LOCAL, LOCAL), BF16),
        t_low=((LOCAL, LOCAL), BF16),
        l_high=((LOCAL, LOCAL), BF16),
        l_low=((LOCAL, LOCAL), BF16),
        e_high=((2 * H * ES, LOCAL), BF16),
        e_low=((2 * H * ES, LOCAL), BF16),
        bw=((2 * SUB, LOCAL), BF16),
        spread=((LANES, LOCAL), F32),
        x_high=((LOCAL, COLS), BF16),
        x_low=((LOCAL, COLS), BF16),
        field=((LANES, LANES), F32),
        cfield=((ES, LANES), F32),
        cst=((3, TALL, LANES), F32),
        cond=((RP, LANES), F32),
        wt=((5, LOCAL, LANES), F32),
        gd=((HV, RP, LANES), F32),
        sol=((HV, CS, ES, LANES), F32),
        res=((HV, LOCAL, LANES), F32),
        img=((HV, CS, ES, LANES), F32),
        aux=((LOCAL, LANES), F32),
        daux=((RP, LANES), F32),
        phi=((RP, PK), BF16),
        wdeep=((HV, RP, LANES), F32),
        deep=((2, HV, RP, LANES), F32),
        kmat=((2, LANES, N * W * SUB), BF16),
        k0=((N, W, K0, COLS), F32),
        g=((ITERS + 1, N, W, SUB, COLS), F32),
        gs_col=((2, CS, COLS), F32),
        g_row=((2, CS, COLS), F32),
        g_col=((2, CS, COLS), F32),
        c_row=((2, ES, LANES), F32),
        c_col=((2, SUB, LANES), F32),
        c_cor=((4, SUB, LANES), F32),
        as_col=((2, H, ES, LANES), F32),
        a_row=((2, H * ES, LANES), F32),
        a_col=((2, H, ES, LANES), F32),
        a_cor=((4, H, SUB, LANES), F32),
        rs_row=((2, HV, OV * ES, LANES), F32),
        rs_col=((2, HV, OV, ES, LANES), F32),
        rs_cor=((4, HV, SUB, LANES), F32),
        r_row=((2, HV, OV * ES, LANES), F32),
        r_col=((2, HV, OV, ES, LANES), F32),
        r_cor=((4, HV, SUB, LANES), F32),
        zs_row=((ITERS, 2, HV, H, ES, LANES), F32),
        zs_col=((ITERS, 2, HV, H, ES, LANES), F32),
        zs_cor=((ITERS, 4, HV, SUB, LANES), F32),
        z_row=((ITERS, 2, HV, H, ES, LANES), F32),
        z_col=((ITERS, 2, HV, H, ES, LANES), F32),
        z_cor=((ITERS, 4, HV, SUB, LANES), F32),
    )
    shapes = {name: pltpu.VMEM(*spec) for name, spec in scratch.items()}
    dma = pltpu.SemaphoreType.DMA
    shapes |= dict(
        ssem=dma((ITERS + 4, 8)),
        rsem=dma((ITERS + 4, 8)),
        gs=dma((ITERS + 2, CHIPS)),
        gr=dma((ITERS + 2, CHIPS)),
        fs=dma((ITERS + 2, CHIPS)),
        fr=dma((ITERS + 2, CHIPS)),
        lsem=dma,
    )
    anywhere = pl.BlockSpec(memory_space=pl.ANY)
    smem = pl.BlockSpec(memory_space=pltpu.SMEM)
    return pl.pallas_call(
        functools.partial(kernel, (N, W, ES, OV, CS, COLS, MODES, KR), tuple(shapes)),
        out_shape=(jax.ShapeDtypeStruct(right_side.shape, F32),) * 2,
        in_specs=[vmem] * 3 + [smem, vmem, anywhere] + [vmem] * 2,
        out_specs=(vmem, vmem),
        scratch_shapes=list(shapes.values()),
        compiler_params=pltpu.CompilerParams(
            collective_id=0, has_side_effects=True, vmem_limit_bytes=60 * 1024 * 1024
        ),
        name="schwarz",
    )(
        right_side,
        initial_guess,
        class_map,
        class_conductivity,
        window_index[0],
        local_inverse[0, 0],
        coarse_basis,
        coarse_inverse,
    )


def solution(mesh):
    in_specs = (
        P("narrow", "wide", None),
        P("narrow", "wide", None),
        P("narrow", "wide"),
        P(),
        P("narrow", "wide", None),
        P("narrow", "wide", None, None),
        P("narrow", "wide", None, None),
        P("wide", "narrow"),
    )
    out_specs = (P("narrow", "wide", None), P("narrow", "wide", None))
    body = functools.partial(local, mesh.shape["narrow"], mesh.shape["wide"])
    return jax.shard_map(body, mesh=mesh, in_specs=in_specs, out_specs=out_specs, check_vma=False)
```

```python
import functools
import math
import types

import jax
import jax.numpy as jnp
from jax import lax
from jax.experimental import pallas as pl
from jax.experimental.pallas import tpu as pltpu
from jax.sharding import PartitionSpec as P

ITERS = 3
REACTION = 0.01
LANES = 128
SUB = 8
F32 = jnp.float32
BF16 = jnp.bfloat16
MESH = pl.DeviceIdType.MESH
DIRS = ((-1, -1), (-1, 0), (-1, 1), (0, -1), (0, 1), (1, -1), (1, 0), (1, 1))

SIDES = (3, 4, 0, 2, 5, 7)
ENDS = (1, 6)


def split(value):
    high = value.astype(BF16)
    return high, (value - high.astype(F32)).astype(BF16)


def dot(left, right):
    return jnp.dot(left, right, preferred_element_type=F32)


def dot3(left_high, left_low, right_high, right_low):
    return dot(left_high, right_high) + (dot(left_low, right_high) + dot(left_high, right_low))


def half(h):
    return slice(h * LANES, (h + 1) * LANES)


def kernel(cfg, names, *refs):
    N, W, ES, OV, CS, COLS, MODES, KR = cfg
    rhs_ref, guess_ref, map_ref, class_ref, wrow_ref, inv_hbm, basis_ref, coarse_ref = refs[:8]
    sol_out, res_out = refs[8:10]
    s = types.SimpleNamespace(**dict(zip(names, refs[10:])))
    H = OV + 1
    lo, hi = OV, OV + CS - H
    LOCAL = ES * ES
    DW = ES + 2
    RP = s.daux.shape[0]
    HV = COLS // LANES
    LK = 3 * MODES * N
    HALF = N // 2
    CHIPS = HALF * W
    base = hi - (ES - SUB)
    a = lax.axis_index("narrow")
    b = lax.axis_index("wide")
    core = lax.rem(a, 2)
    me = (a // 2) * W + b

    def at(u, t):
        return (u + 1) * DW + t + 1

    def other(k):
        idx = lax.rem(me + k, CHIPS)
        return idx, (lax.rem(idx, W), 2 * (idx // W) + core)

    def valid(d):
        da, db = DIRS[d]
        return (a + da >= 0) & (a + da < N) & (b + db >= 0) & (b + db < W)

    barrier = pltpu.get_barrier_semaphore()

    def greet(k, carry):
        pl.semaphore_signal(barrier, inc=1, device_id=other(k)[1], device_id_type=MESH)
        return carry

    lax.fori_loop(1, CHIPS, greet, 0)
    count = CHIPS - 1
    for d, (da, db) in enumerate(DIRS):
        if da != 0:
            ok = valid(d)
            count = count + ok.astype(jnp.int32)

            @pl.when(ok)
            def _():
                pl.semaphore_signal(barrier, inc=1, device_id=(b + db, a + da), device_id_type=MESH)

    load = pltpu.make_async_copy(inv_hbm, s.inv, s.lsem)
    load.start()

    def landing(d, rows, cols, corners, away):
        da, db = DIRS[d]
        if away:
            da, db = -da, -db
        if db == 0:
            return rows((da + 1) // 2)
        if da == 0:
            return cols((db + 1) // 2)
        return corners((da + 1) + (db + 1) // 2)

    groups = [
        (s.g_row, s.g_col, None),
        (s.c_row, s.c_col, s.c_cor),
        (s.a_row, s.a_col, s.a_cor),
        (s.r_row, s.r_col, s.r_cor),
    ]
    groups += [(s.z_row.at[i], s.z_col.at[i], s.z_cor.at[i]) for i in range(ITERS)]

    for d in range(8):

        @pl.when(jnp.logical_not(valid(d)))
        def _():
            for rows, cols, corners in groups:
                if corners is None and 0 not in DIRS[d]:
                    continue
                pick = lambda ref: lambda i: ref.at[i]
                ref = landing(d, pick(rows), pick(cols), corners is not None and pick(corners), False)
                ref[...] = jnp.zeros(ref.shape, F32)

    def exchange(slot, rows, cols, corners):
        copies = {}
        lane = slot if slot < 4 else 4 + slot % 2
        for d in range(8):
            if corners is None and 0 not in DIRS[d]:
                continue
            da, db = DIRS[d]
            to = groups[slot]
            pick = lambda ref: lambda i: ref.at[i]
            copies[d] = pltpu.make_async_remote_copy(
                src_ref=landing(d, rows, cols, corners, False),
                dst_ref=landing(d, pick(to[0]), pick(to[1]), to[2] is not None and pick(to[2]), True),
                send_sem=s.ssem.at[lane, d],
                recv_sem=s.rsem.at[lane, 7 - d],
                device_id=(b + db, a + da),
                device_id_type=MESH,
            )
        return copies

    def send(copies, dirs=SIDES + ENDS):
        for d in dirs:
            if d in copies:

                @pl.when(valid(d))
                def _():
                    copies[d].start()

    def recv(copies):
        for d in copies:

            @pl.when(valid(d))
            def _():
                copies[7 - d].wait_recv()

    def done(copies):
        for d in copies:

            @pl.when(valid(d))
            def _():
                copies[d].wait_send()

    def place_of(slot):
        return 2 if slot == 0 else (slot - 1) % 2

    def gather_copy(slot, k, ref, rows):
        slot = place_of(slot)
        _, target = other(k)
        part = ref.at[a, b, rows]
        return pltpu.make_async_remote_copy(
            src_ref=part,
            dst_ref=part,
            send_sem=s.gs.at[slot, k],
            recv_sem=s.gr.at[slot, me],
            device_id=target,
            device_id_type=MESH,
        )

    def forward(slot, k, ref, rows, mine):
        slot = place_of(slot)
        idx, _ = other(k)
        row = 2 * (idx // W)
        part = ref.at[row + core, lax.rem(idx, W), rows]
        away = part if mine else ref.at[row + 1 - core, lax.rem(idx, W), rows]
        return pltpu.make_async_remote_copy(
            src_ref=part,
            dst_ref=away,
            send_sem=s.fs.at[slot, k],
            recv_sem=s.fr.at[slot, idx],
            device_id=(b, a + 1 - 2 * core),
            device_id_type=MESH,
        )

    def gather_send(slot, ref, rows):
        if CHIPS <= 16:
            for k in range(1, CHIPS):
                gather_copy(slot, k, ref, rows).start()
        else:

            def body(k, carry):
                gather_copy(slot, k, ref, rows).start()
                return carry

            lax.fori_loop(1, CHIPS, body, 0)
        forward(slot, 0, ref, rows, True).start()

    def gather_recv(slot, ref, rows):
        def relay(k, carry):
            idx, target = other(k)
            pltpu.make_async_remote_copy(
                src_ref=ref.at[a, b, rows],
                dst_ref=ref.at[target[1], target[0], rows],
                send_sem=s.gs.at[place_of(slot), k],
                recv_sem=s.gr.at[place_of(slot), idx],
                device_id=target,
                device_id_type=MESH,
            ).wait_recv()
            forward(slot, k, ref, rows, True).start()
            return carry

        lax.fori_loop(1, CHIPS, relay, 0)

        def collect(k, carry):
            forward(slot, k, ref, rows, False).wait_recv()
            return carry

        lax.fori_loop(0, CHIPS, collect, 0)

    def gather_done(slot, ref, rows):
        def body(k, carry):
            gather_copy(slot, k, ref, rows).wait_send()
            return carry

        lax.fori_loop(1, CHIPS, body, 0)

        def sent(k, carry):
            forward(slot, k, ref, rows, True).wait_send()
            return carry

        lax.fori_loop(0, CHIPS, sent, 0)

    def edges_of_guess(i, carry):
        s.gs_col[0, pl.ds(i, 1), :] = guess_ref[i, 0:1, :]
        s.gs_col[1, pl.ds(i, 1), :] = guess_ref[i, CS - 1 : CS, :]
        return carry

    lax.fori_loop(0, CS, edges_of_guess, 0)
    classes = map_ref[...]
    conduct = jnp.zeros(classes.shape, F32)
    for k in range(class_ref.shape[0]):
        conduct = jnp.where(classes == k, class_ref[k], conduct)
    s.field[...] = jnp.zeros(s.field.shape, F32)
    s.field[0:CS, 0:CS] = conduct
    s.cfield[...] = jnp.transpose(s.field[...])[0:ES]
    run = MODES * W
    for i in range(MODES * N):
        line, left = divmod(i * run, COLS)
        s.k0[a, b, line : line + 1, left : left + run] = coarse_ref[i : i + 1]

    guess_sends = exchange(
        0, lambda i: guess_ref.at[i * (CS - 1)], lambda i: s.gs_col.at[i], None
    )
    tile = lambda i: s.cfield.at[pl.ds(i * (ES - SUB), SUB)]
    cond_sends = exchange(1, lambda i: s.cfield, tile, lambda i: tile(i % 2))
    pl.semaphore_wait(barrier, count)
    send(cond_sends)
    send(guess_sends)
    k_rows = pl.ds(0, KR)
    gather_send(0, s.k0, k_rows)

    step = 256
    numbering = wrow_ref[...]
    tall_numbering = jnp.transpose(jnp.broadcast_to(numbering, (LANES, LOCAL)))
    lane = lax.broadcasted_iota(jnp.int32, (LOCAL, LANES), 1)
    for c in range(0, LOCAL, LANES):
        s.perm_t[:, c : c + LANES] = jnp.where(lane + c == tall_numbering, 1.0, 0.0).astype(BF16)

    NE = 2 * H * ES
    line = lax.broadcasted_iota(jnp.int32, (NE, LOCAL), 0)
    col = line >> int(math.log2(ES))
    col = jnp.where(col < H, col + lo, col - H + hi)
    pos = (line & (ES - 1)) * ES + col
    s.perm[0:NE, :] = jnp.where(pos == numbering, 1.0, 0.0).astype(BF16)

    def hot(i, carry):
        off = pl.multiple_of(i * step, step)
        pos = lax.broadcasted_iota(jnp.int32, (step, LOCAL), 0) + off
        s.perm[pl.ds(NE + off, step), :] = jnp.where(pos == numbering, 1.0, 0.0).astype(BF16)
        return carry

    lax.fori_loop(0, LOCAL // step, hot, 0)
    basis = basis_ref[0, 0]
    place = lax.rem(b, 3) * (MODES * N) + a * MODES
    line = lax.broadcasted_iota(jnp.int32, (LANES, LOCAL), 0) - place
    s.spread[...] = jnp.zeros(s.spread.shape, F32)
    for m in range(MODES):
        s.spread[...] = jnp.where(line == m, basis[m : m + 1], s.spread[...])
    b_high, b_low = split(jnp.transpose(s.spread[...]))
    both = dot(s.perm[NE:, :], jnp.concatenate([b_high, b_low], axis=1))
    s.aux[...] = both[:, 0:LANES] + both[:, LANES:]
    for k, first in enumerate((lo, hi)):
        for j in range(H):
            s.as_col[k, j] = s.aux[pl.ds(first + j, ES, stride=ES), :]
    aux_sends = exchange(
        2,
        lambda i: s.aux.at[pl.ds((lo, hi)[i] * ES, H * ES)],
        lambda i: s.as_col.at[i],
        lambda i: s.as_col.at[i % 2, pl.ds(0, H), pl.ds((ES - SUB) * (i // 2), SUB)],
    )

    def place_guess(i, carry):
        for h in range(HV):
            s.gd[h, pl.ds(at(OV + i, OV), CS), :] = guess_ref[i, :, half(h)]
            s.sol[h, i, 0:CS, :] = guess_ref[i, :, half(h)]
        return carry

    lax.fori_loop(0, CS, place_guess, 0)
    recv(guess_sends)
    recv(cond_sends)
    for h in range(HV):
        for side in range(2):
            edge = OV - 1 + side * (CS + 1)
            s.gd[h, pl.ds(at(edge, OV), CS), :] = s.g_row[side, :, half(h)]
            s.gd[h, pl.ds(at(OV, edge), CS, stride=DW), :] = s.g_col[side, :, half(h)]
    stack = (
        (s.c_cor.at[0], s.c_row.at[0], s.c_cor.at[1]),
        (s.c_col.at[0], s.cfield, s.c_col.at[1]),
        (s.c_cor.at[2], s.c_row.at[1], s.c_cor.at[3]),
    )
    for k, (left, mid, right) in enumerate(stack):
        s.cst[k, 0:H] = left[CS - H - (ES - SUB) : CS - (ES - SUB)]
        s.cst[k, H : H + CS] = mid[0:CS]
        s.cst[k, H + CS : DW] = right[0:H]
    clane = lax.broadcasted_iota(jnp.int32, s.cst.shape[1:], 1)
    cmap = jnp.where(
        clane < H,
        pltpu.roll(s.cst[0], LANES - (CS - H), 1),
        jnp.where(
            clane < H + CS, pltpu.roll(s.cst[1], H, 1), pltpu.roll(s.cst[2], H + CS, 1)
        ),
    )
    for r in range(DW):
        s.cond[pl.ds(r * DW, DW), :] = jnp.broadcast_to(cmap[0:DW, r : r + 1], (DW, LANES))
    col_pos = b * CS - OV + lax.broadcasted_iota(jnp.int32, (ES, LANES), 0)
    col_in = jnp.where((col_pos >= 0) & (col_pos < CS * W), 1.0, 0.0)

    def faces(u, carry):
        row_pos = a * CS - OV + u
        inside = jnp.where((row_pos >= 0) & (row_pos < CS * N), col_in, 0.0)
        cond = lambda du, dt: s.cond[pl.ds(at(u + du, dt), ES), :]
        own = cond(0, 0)
        halved = 0.5 * inside
        parts = [halved * (own + cond(*o)) for o in ((-1, 0), (1, 0), (0, -1), (0, 1))]
        here = pl.ds(pl.multiple_of(u * ES, ES), ES)
        s.wt[0, here, :] = REACTION * inside + ((parts[0] + parts[1]) + (parts[2] + parts[3]))
        for k in range(4):
            s.wt[1 + k, here, :] = parts[k]
        return carry

    lax.fori_loop(0, ES, faces, 0)

    def operator(read, u, t, n):
        weights = [s.wt[k, pl.ds(u * ES + t, n), :] for k in range(5)]
        out = []
        for h in range(HV):
            v = lambda du, dt: read(h, pl.ds(at(u + du, t + dt), n))
            around = weights[1] * v(-1, 0) + weights[2] * v(1, 0)
            beside = weights[3] * v(0, -1) + weights[4] * v(0, 1)
            out.append(weights[0] * v(0, 0) - (around + beside))
        return out

    def own_residual(i, carry):
        u = OV + i
        image = operator(lambda h, rows: s.gd[h, rows, :], u, OV, CS)
        for h in range(HV):
            s.res[h, pl.ds(u * ES + OV, CS), :] = rhs_ref[i, :, half(h)] - image[h]
        return carry

    lax.fori_loop(0, CS, own_residual, 0)

    near = (OV, CS)
    for k in range(2):
        for h in range(HV):
            for q in range(OV):
                s.rs_col[k, h, q] = s.res[h, pl.ds(near[k] + q, ES, stride=ES), :]
            s.rs_row[k, h] = s.res[h, near[k] * ES : (near[k] + OV) * ES, :]
    for k in range(4):
        for h in range(HV):
            for r in range(OV):
                cell = (near[k // 2] + r) * ES + near[k % 2]
                s.rs_cor[k, h, r * OV : (r + 1) * OV, :] = s.res[h, cell : cell + OV, :]
    res_sends = exchange(
        3,
        lambda i: s.rs_row.at[i],
        lambda i: s.rs_col.at[i],
        lambda i: s.rs_cor.at[i],
    )
    send(res_sends)
    send(aux_sends)

    load.wait()

    def right_side_perm(i, carry):
        rows = pl.ds(pl.multiple_of(i * step, step), step)
        high, low = split(s.inv[rows, :])
        both = dot(jnp.concatenate([high, low], axis=0), s.perm_t[...]).astype(BF16)
        s.t_high[rows, :] = both[0:step]
        s.t_low[rows, :] = both[step:]
        return carry

    lax.fori_loop(0, LOCAL // step, right_side_perm, 0)
    m_high, m_low = split(jnp.concatenate([basis, jnp.zeros((SUB - MODES, LOCAL), F32)], axis=0))
    s.bw[...] = dot(jnp.concatenate([m_high, m_low], axis=0), s.perm_t[...]).astype(BF16)

    def set_x(u, value):
        high, low = split(jnp.concatenate(value, axis=1))
        rows = pl.ds(pl.multiple_of(u * ES, ES), ES)
        s.x_high[rows, :] = high
        s.x_low[rows, :] = low

    recv(res_sends)
    far = (0, OV + CS)
    for h in range(HV):
        for k in range(2):
            for q in range(OV):
                line = slice(q * ES + OV, q * ES + OV + CS)
                s.res[h, pl.ds((far[k] + q) * ES + OV, CS), :] = s.r_row[k, h, line, :]
                line = pl.ds(OV * ES + far[k] + q, CS, stride=ES)
                s.res[h, line, :] = s.r_col[k, h, q, OV : OV + CS, :]
        for k in range(4):
            for r in range(OV):
                cell = (far[k // 2] + r) * ES + far[k % 2]
                s.res[h, cell : cell + OV, :] = s.r_cor[k, h, r * OV : (r + 1) * OV, :]

    def first_x(u, carry):
        set_x(u, [s.res[h, pl.ds(u * ES, ES), :] for h in range(HV)])
        return carry

    lax.fori_loop(0, ES, first_x, 0)

    def coarse_rows():
        both = dot(s.bw[...], s.x_high[...])
        return both[0:SUB] + (both[SUB:] + dot(s.bw[0:SUB, :], s.x_low[...]))

    def left_side_perm(i, carry):
        big = (NE + LOCAL) // 2
        rows = pl.ds(pl.multiple_of(i * big, big), big)
        s.l_high[rows, :] = dot(s.perm[rows, :], s.t_high[...]).astype(BF16)
        s.l_low[rows, :] = dot(s.perm[rows, :], s.t_low[...]).astype(BF16)
        return carry

    def build_phi():
        recv(aux_sends)
        for i in range(CS):
            s.daux[pl.ds(at(OV + i, OV), CS), :] = s.aux[pl.ds((OV + i) * ES + OV, CS), :]
        for k in range(2):
            for j in range(H):
                deep_line = k * (CS + H) + j
                s.daux[pl.ds(deep_line * DW + H, CS), :] = s.a_row[
                    k, j * ES + OV : j * ES + OV + CS, :
                ]
                s.daux[pl.ds(H * DW + deep_line, CS, stride=DW), :] = s.a_col[
                    k, j, OV : OV + CS, :
                ]
        for k in range(4):
            first = lo if k // 2 else base
            for q in range(H):
                cell = (k // 2) * (CS + H) * DW + (k % 2) * (CS + H) + q
                for r in range(H):
                    s.daux[pl.ds(cell + r * DW, 1), :] = s.a_cor[k, q, first + r : first + r + 1, :]
        chunk = RP // 2

        def body(i, carry):
            rows = pl.ds(pl.multiple_of(i * chunk, chunk), chunk)
            value = s.daux[rows, :]
            high = value.astype(BF16).astype(F32)
            low = value - high
            if 2 * LK <= LANES:
                s.phi[rows, 0:LANES] = (high + pltpu.roll(low, LK, 1)).astype(BF16)
                s.phi[rows, LANES:] = high.astype(BF16)
            else:
                s.phi[rows, 0:LANES] = high.astype(BF16)
                s.phi[rows, LANES : 2 * LANES] = low.astype(BF16)
                s.phi[rows, 2 * LANES :] = high.astype(BF16)
            return carry

        lax.fori_loop(0, 2, body, 0)

    def build_kmat():
        gather_recv(0, s.k0, k_rows)
        per = COLS // (4 * W)
        wide_cols = MODES * W
        group = MODES * N
        piece = lax.broadcasted_iota(jnp.int32, (group, COLS), 0) & (per - 1)
        lane = lax.broadcasted_iota(jnp.int32, (group, COLS), 1)
        keep = (lane >> int(math.log2(wide_cols))) == piece
        width = N * W * SUB
        j = lax.broadcasted_iota(jnp.int32, (COLS, width), 0) & (wide_cols - 1)
        c = lax.broadcasted_iota(jnp.int32, (COLS, width), 1)
        total_high = total_low = None
        for a2 in range(N):
            blocks = []
            for third in range(3):
                db = lax.rem(third - b + 1 + 3 * W, 3) - 1
                spot = jnp.clip(b + db, 0, W - 1)
                raw = s.k0[a2, spot, 0:KR, :]
                tall = jnp.concatenate(
                    [jnp.broadcast_to(raw[r : r + 1], (per, COLS)) for r in range(KR)], axis=0
                )
                blocks.append(jnp.where(keep, tall, 0.0))
            if 2 * LK <= LANES:
                blocks = blocks * 2
            fill = LANES - len(blocks) * group
            blocks.append(jnp.zeros((fill, COLS), F32))
            high, low = split(jnp.concatenate(blocks, axis=0))
            fold = c == a2 * (W * SUB) + (j >> 2) * SUB + (j & 3)
            fold = jnp.where(fold, 1.0, 0.0).astype(BF16)
            th, tl = dot(high, fold), dot(low, fold)
            total_high = th if total_high is None else total_high + th
            total_low = tl if total_low is None else total_low + tl
        s.kmat[0] = total_high.astype(BF16)
        s.kmat[1] = total_low.astype(BF16)

    sub_pos = lax.broadcasted_iota(jnp.int32, (SUB, COLS), 0)
    pending = [guess_sends, cond_sends, aux_sends, res_sends]
    numer = denom = None
    sizes = []
    spans = []
    for it in range(ITERS + 1):
        ref = s.g.at[it]
        first = MODES if it == ITERS else 0
        last = MODES if it == 0 else MODES + 2
        span = pl.ds(first, last - first)
        spans.append(span)
        rows = coarse_rows() if it < ITERS else jnp.zeros((SUB, COLS), F32)
        if it > 0:
            rows = jnp.where(sub_pos == MODES, numer, rows)
            rows = jnp.where(sub_pos == MODES + 1, denom, rows)
        ref[a, b] = rows
        gather_send(it + 1, ref, span)
        if it < ITERS:
            if it == 0:
                left_side_perm(0, 0)
            value = dot3(s.l_high[0:NE, :], s.l_low[0:NE, :], s.x_high[...], s.x_low[...])
            for k in range(2):
                for j in range(H):
                    line = (k * H + j) * ES
                    for h in range(HV):
                        s.zs_col[it, k, h, j] = value[line : line + ES, half(h)]
            for k in range(4):
                u0 = hi if k // 2 else lo
                skip = ((H - 1) * (k // 2), (H - 1) * (k % 2))
                n = 0
                for r in range(H):
                    for j in range(H):
                        if (r, j) == ((H - 1) - skip[0], (H - 1) - skip[1]):
                            continue
                        for h in range(HV):
                            s.zs_cor[it, k, h, n : n + 1, :] = s.zs_col[
                                it, k % 2, h, j, u0 + r : u0 + r + 1, :
                            ]
                        n += 1
            copies = exchange(
                4 + it,
                lambda i: s.zs_row.at[it, i],
                lambda i: s.zs_col.at[it, i],
                lambda i: s.zs_cor.at[it, i],
            )
            send(copies, SIDES)
            if it == 0:
                left_side_perm(1, 0)

            def solve(i, carry):
                rows = pl.ds(NE + pl.multiple_of(i * step, step), step)
                value = dot3(s.l_high[rows, :], s.l_low[rows, :], s.x_high[...], s.x_low[...])
                for j in range(step // ES):
                    u = i * (step // ES) + j
                    for h in range(HV):
                        s.wdeep[h, pl.ds(at(u, 0), ES), :] = value[j * ES : (j + 1) * ES, half(h)]
                return carry

            lax.fori_loop(0, LOCAL // step, solve, 0)
            for k, u in enumerate((lo, hi)):
                for h in range(HV):
                    for r in range(H):
                        s.zs_row[it, k, h, r] = s.wdeep[h, pl.ds(at(u + r, 0), ES), :]
            send(copies, ENDS)
            pending.append(copies)
        if it == 0:
            build_phi()
            build_kmat()
            for early in pending[0:4]:
                done(early)
            gather_done(0, s.k0, k_rows)
        else:
            done(pending[3 + it])
            gather_done(it, s.g.at[it - 1], spans[it - 1])
        if it >= 2:
            old = sizes[it - 2]

            def advance(i, carry):
                for h in range(HV):
                    here = s.deep[it % 2, h, pl.ds(at(OV + i, OV), CS), :]
                    s.sol[h, i, 0:CS, :] = s.sol[h, i, 0:CS, :] + old[:, half(h)] * here
                return carry

            lax.fori_loop(0, CS, advance, 0)
        gather_recv(it + 1, ref, span)
        everyone = ref[...].reshape(N * W, SUB, COLS)
        if it > 0:
            total = jnp.sum(everyone, axis=0)
            size = total[MODES : MODES + 1] / total[MODES + 1 : MODES + 2]
            sizes.append(size)
        if it == ITERS:
            break
        coarse_only = lax.broadcasted_iota(jnp.int32, everyone.shape, 1) < MODES
        everyone = jnp.where(coarse_only, everyone, 0.0)
        g_high, g_low = split(everyone.reshape(N * W * SUB, COLS))
        s_high, s_low = split(dot3(s.kmat[0], s.kmat[1], g_high, g_low))
        if 2 * LK <= LANES:
            s_all = jnp.concatenate([s_high, s_low], axis=0)
        else:
            s_all = jnp.concatenate([s_high, s_high, s_low], axis=0)
        recv(copies)
        for h in range(HV):
            for k in range(2):
                for j in range(H):
                    deep_line = k * (CS + H) + j
                    s.wdeep[h, pl.ds(deep_line * DW + H, CS), :] = s.z_row[
                        it, k, h, j, OV : OV + CS, :
                    ]
                    s.wdeep[h, pl.ds(H * DW + deep_line, CS, stride=DW), :] = s.z_col[
                        it, k, h, j, OV : OV + CS, :
                    ]
            for k in range(4):
                skip = ((H - 1) * (k // 2), (H - 1) * (k % 2))
                n = 0
                for r in range(H):
                    for j in range(H):
                        if (r, j) == skip:
                            continue
                        cell = ((k // 2) * (CS + H) + r) * DW + (k % 2) * (CS + H) + j
                        s.wdeep[h, pl.ds(cell, 1), :] = s.z_cor[it, k, h, n : n + 1, :]
                        n += 1
        chunk = RP // 2
        now, before = it % 2, 1 - it % 2

        def coarse_part(i, carry):
            rows = pl.ds(pl.multiple_of(i * chunk, chunk), chunk)
            value = dot(s.phi[rows, :], s_all)
            for h in range(HV):
                part = value[:, half(h)] + s.wdeep[h, rows, :]
                if it > 0:
                    part = s.deep[before, h, rows, :] - size[:, half(h)] * part
                s.deep[now, h, rows, :] = part
            return carry

        lax.fori_loop(0, 2, coarse_part, 0)
        read = lambda h, rows: s.deep[now, h, rows, :]
        if it < ITERS - 1:

            def margin(q, carry):
                u = jnp.where(q < OV, q, q + CS)
                set_x(u, operator(read, u, 0, ES))
                return carry

            lax.fori_loop(0, 2 * OV, margin, 0)

        def apply(i, carry):
            u = OV + i
            value = operator(read, u, 0, ES)
            if it < ITERS - 1:
                set_x(u, value)
            line = pl.ds(pl.multiple_of(u * ES, ES), ES)
            sums = []
            for h in range(HV):
                left = s.res[h, line, :]
                if it > 0:
                    left = left - size[:, half(h)] * s.img[h, i]
                    s.res[h, line, :] = left
                s.img[h, i] = value[h]
                sums.append(carry[2 * h] + left * value[h])
                sums.append(carry[2 * h + 1] + value[h] * value[h])
            return tuple(sums)

        nothing = jnp.zeros((ES, LANES), F32)
        sums = lax.fori_loop(0, CS, apply, (nothing,) * (2 * HV))
        col = lax.broadcasted_iota(jnp.int32, (ES, LANES), 0)
        mine = (col >= OV) & (col < OV + CS)
        sums = [jnp.sum(jnp.where(mine, v, 0.0), axis=0, keepdims=True) for v in sums]
        numer = jnp.concatenate(sums[0::2], axis=1)
        denom = jnp.concatenate(sums[1::2], axis=1)

    size = sizes[-1]

    def finish(i, carry):
        u = OV + i
        for h in range(HV):
            step_of = size[:, half(h)]
            here = s.deep[(ITERS - 1) % 2, h, pl.ds(at(u, OV), CS), :]
            sol_out[i, :, half(h)] = s.sol[h, i, 0:CS, :] + step_of * here
            here = s.img[h, i, OV : OV + CS, :]
            res_out[i, :, half(h)] = s.res[h, pl.ds(u * ES + OV, CS), :] - step_of * here
        return carry

    lax.fori_loop(0, CS, finish, 0)
    gather_done(ITERS + 1, s.g.at[ITERS], spans[ITERS])


def local(
    N,
    W,
    right_side,
    initial_guess,
    class_map,
    class_conductivity,
    window_index,
    local_inverse,
    coarse_basis,
    coarse_inverse,
):
    CS, _, COLS = right_side.shape
    MODES, LOCAL = coarse_basis.shape[2:]
    ES = math.isqrt(LOCAL)
    OV = (ES - CS) // 2
    H = OV + 1
    DW = ES + 2
    RP = -(-DW * DW // 32) * 32
    HV = COLS // LANES
    KR = coarse_inverse.size // COLS
    K0 = -(-KR // SUB) * SUB
    CHIPS = N * W // 2
    PK = (2 if 6 * MODES * N <= LANES else 3) * LANES
    TALL = -(-DW // SUB) * SUB
    vmem = pl.BlockSpec(memory_space=pltpu.VMEM)
    scratch = dict(
        inv=((LOCAL, LOCAL), F32),
        perm=((2 * H * ES + LOCAL, LOCAL), BF16),
        perm_t=((LOCAL, LOCAL), BF16),
        t_high=((LOCAL, LOCAL), BF16),
        t_low=((LOCAL, LOCAL), BF16),
        l_high=((2 * H * ES + LOCAL, LOCAL), BF16),
        l_low=((2 * H * ES + LOCAL, LOCAL), BF16),
        bw=((2 * SUB, LOCAL), BF16),
        spread=((LANES, LOCAL), F32),
        x_high=((LOCAL, COLS), BF16),
        x_low=((LOCAL, COLS), BF16),
        field=((LANES, LANES), F32),
        cfield=((ES, LANES), F32),
        cst=((3, TALL, LANES), F32),
        cond=((RP, LANES), F32),
        wt=((5, LOCAL, LANES), F32),
        gd=((HV, RP, LANES), F32),
        sol=((HV, CS, ES, LANES), F32),
        res=((HV, LOCAL, LANES), F32),
        img=((HV, CS, ES, LANES), F32),
        aux=((LOCAL, LANES), F32),
        daux=((RP, LANES), F32),
        phi=((RP, PK), BF16),
        wdeep=((HV, RP, LANES), F32),
        deep=((2, HV, RP, LANES), F32),
        kmat=((2, LANES, N * W * SUB), BF16),
        k0=((N, W, K0, COLS), F32),
        g=((ITERS + 1, N, W, SUB, COLS), F32),
        gs_col=((2, CS, COLS), F32),
        g_row=((2, CS, COLS), F32),
        g_col=((2, CS, COLS), F32),
        c_row=((2, ES, LANES), F32),
        c_col=((2, SUB, LANES), F32),
        c_cor=((4, SUB, LANES), F32),
        as_col=((2, H, ES, LANES), F32),
        a_row=((2, H * ES, LANES), F32),
        a_col=((2, H, ES, LANES), F32),
        a_cor=((4, H, SUB, LANES), F32),
        rs_row=((2, HV, OV * ES, LANES), F32),
        rs_col=((2, HV, OV, ES, LANES), F32),
        rs_cor=((4, HV, SUB, LANES), F32),
        r_row=((2, HV, OV * ES, LANES), F32),
        r_col=((2, HV, OV, ES, LANES), F32),
        r_cor=((4, HV, SUB, LANES), F32),
        zs_row=((ITERS, 2, HV, H, ES, LANES), F32),
        zs_col=((ITERS, 2, HV, H, ES, LANES), F32),
        zs_cor=((ITERS, 4, HV, SUB, LANES), F32),
        z_row=((ITERS, 2, HV, H, ES, LANES), F32),
        z_col=((ITERS, 2, HV, H, ES, LANES), F32),
        z_cor=((ITERS, 4, HV, SUB, LANES), F32),
    )
    shapes = {name: pltpu.VMEM(*spec) for name, spec in scratch.items()}
    dma = pltpu.SemaphoreType.DMA
    shapes |= dict(
        ssem=dma((6, 8)),
        rsem=dma((6, 8)),
        gs=dma((3, CHIPS)),
        gr=dma((3, CHIPS)),
        fs=dma((3, CHIPS)),
        fr=dma((3, CHIPS)),
        lsem=dma,
    )
    anywhere = pl.BlockSpec(memory_space=pl.ANY)
    smem = pl.BlockSpec(memory_space=pltpu.SMEM)
    fields = pl.pallas_call(
        functools.partial(kernel, (N, W, ES, OV, CS, COLS, MODES, KR), tuple(shapes)),
        out_shape=(pltpu.VMEM(right_side.shape, F32),) * 2,
        in_specs=[vmem] * 3 + [smem, vmem, anywhere] + [vmem] * 2,
        out_specs=(vmem, vmem),
        scratch_shapes=list(shapes.values()),
        compiler_params=pltpu.CompilerParams(
            collective_id=0, has_side_effects=True, vmem_limit_bytes=60 * 1024 * 1024
        ),
        name="schwarz",
    )(
        right_side,
        initial_guess,
        class_map,
        class_conductivity,
        window_index[0],
        local_inverse[0, 0],
        coarse_basis,
        coarse_inverse,
    )
    return tuple(fields)


def solution(mesh):
    in_specs = (
        P("narrow", "wide", None),
        P("narrow", "wide", None),
        P("narrow", "wide"),
        P(),
        P("narrow", "wide", None),
        P("narrow", "wide", None, None),
        P("narrow", "wide", None, None),
        P("wide", "narrow"),
    )
    out_specs = (P("narrow", "wide", None), P("narrow", "wide", None))
    body = functools.partial(local, mesh.shape["narrow"], mesh.shape["wide"])
    return jax.shard_map(body, mesh=mesh, in_specs=in_specs, out_specs=out_specs, check_vma=False)
```

```python
import functools
import math
import types

import jax
import jax.numpy as jnp
from jax import lax
from jax.experimental import pallas as pl
from jax.experimental.pallas import tpu as pltpu
from jax.sharding import PartitionSpec as P

ITERS = 3
REACTION = 0.01
LANES = 128
SUB = 8
F32 = jnp.float32
BF16 = jnp.bfloat16
MESH = pl.DeviceIdType.MESH
DIRS = ((-1, -1), (-1, 0), (-1, 1), (0, -1), (0, 1), (1, -1), (1, 0), (1, 1))

SIDES = (3, 4, 0, 2, 5, 7)
ENDS = (1, 6)


def split(value):
    high = value.astype(BF16)
    return high, (value - high.astype(F32)).astype(BF16)


def dot(left, right):
    return jnp.dot(left, right, preferred_element_type=F32)


def dot3(left_high, left_low, right_high, right_low):
    return dot(left_high, right_high) + (dot(left_low, right_high) + dot(left_high, right_low))


def half(h):
    return slice(h * LANES, (h + 1) * LANES)


def kernel(cfg, names, *refs):
    N, W, ES, OV, CS, COLS, MODES, KR = cfg
    rhs_ref, guess_ref, map_ref, class_ref, wrow_ref, inv_hbm, basis_ref, coarse_ref = refs[:8]
    sol_out, res_out = refs[8:10]
    s = types.SimpleNamespace(**dict(zip(names, refs[10:])))
    H = OV + 1
    lo, hi = OV, OV + CS - H
    LOCAL = ES * ES
    DW = ES + 2
    RP = s.daux.shape[0]
    HV = COLS // LANES
    LK = 3 * MODES * N
    HALF = N // 2
    CHIPS = HALF * W
    base = hi - (ES - SUB)
    a = lax.axis_index("narrow")
    b = lax.axis_index("wide")
    core = lax.rem(a, 2)
    me = (a // 2) * W + b

    def at(u, t):
        return (u + 1) * DW + t + 1

    def other(k):
        idx = lax.rem(me + k, CHIPS)
        return idx, (lax.rem(idx, W), 2 * (idx // W) + core)

    def valid(d):
        da, db = DIRS[d]
        return (a + da >= 0) & (a + da < N) & (b + db >= 0) & (b + db < W)

    barrier = pltpu.get_barrier_semaphore()

    def greet(k, carry):
        pl.semaphore_signal(barrier, inc=1, device_id=other(k)[1], device_id_type=MESH)
        return carry

    lax.fori_loop(1, CHIPS, greet, 0)
    count = CHIPS - 1
    for d, (da, db) in enumerate(DIRS):
        if da != 0:
            ok = valid(d)
            count = count + ok.astype(jnp.int32)

            @pl.when(ok)
            def _():
                pl.semaphore_signal(barrier, inc=1, device_id=(b + db, a + da), device_id_type=MESH)

    load = pltpu.make_async_copy(inv_hbm, s.inv, s.lsem)
    load.start()

    def landing(d, rows, cols, corners, away):
        da, db = DIRS[d]
        if away:
            da, db = -da, -db
        if db == 0:
            return rows((da + 1) // 2)
        if da == 0:
            return cols((db + 1) // 2)
        return corners((da + 1) + (db + 1) // 2)

    groups = [
        (s.g_row, s.g_col, None),
        (s.c_row, s.c_col, s.c_cor),
        (s.a_row, s.a_col, s.a_cor),
        (s.r_row, s.r_col, s.r_cor),
    ]
    groups += [(s.z_row.at[i], s.z_col.at[i], s.z_cor.at[i]) for i in range(ITERS)]

    for d in range(8):

        @pl.when(jnp.logical_not(valid(d)))
        def _():
            for rows, cols, corners in groups:
                if corners is None and 0 not in DIRS[d]:
                    continue
                pick = lambda ref: lambda i: ref.at[i]
                ref = landing(d, pick(rows), pick(cols), corners is not None and pick(corners), False)
                ref[...] = jnp.zeros(ref.shape, F32)

    def exchange(slot, rows, cols, corners):
        copies = {}
        lane = slot if slot < 4 else 4 + slot % 2
        for d in range(8):
            if corners is None and 0 not in DIRS[d]:
                continue
            da, db = DIRS[d]
            to = groups[slot]
            pick = lambda ref: lambda i: ref.at[i]
            copies[d] = pltpu.make_async_remote_copy(
                src_ref=landing(d, rows, cols, corners, False),
                dst_ref=landing(d, pick(to[0]), pick(to[1]), to[2] is not None and pick(to[2]), True),
                send_sem=s.ssem.at[lane, d],
                recv_sem=s.rsem.at[lane, 7 - d],
                device_id=(b + db, a + da),
                device_id_type=MESH,
            )
        return copies

    def send(copies, dirs=SIDES + ENDS):
        for d in dirs:
            if d in copies:

                @pl.when(valid(d))
                def _():
                    copies[d].start()

    def recv(copies):
        for d in copies:

            @pl.when(valid(d))
            def _():
                copies[7 - d].wait_recv()

    def done(copies):
        for d in copies:

            @pl.when(valid(d))
            def _():
                copies[d].wait_send()

    def place_of(slot):
        return 2 if slot == 0 else (slot - 1) % 2

    def gather_copy(slot, k, ref, rows):
        slot = place_of(slot)
        _, target = other(k)
        part = ref.at[a, b, rows]
        return pltpu.make_async_remote_copy(
            src_ref=part,
            dst_ref=part,
            send_sem=s.gs.at[slot, k],
            recv_sem=s.gr.at[slot, me],
            device_id=target,
            device_id_type=MESH,
        )

    def forward(slot, k, ref, rows, mine):
        slot = place_of(slot)
        idx, _ = other(k)
        row = 2 * (idx // W)
        part = ref.at[row + core, lax.rem(idx, W), rows]
        away = part if mine else ref.at[row + 1 - core, lax.rem(idx, W), rows]
        return pltpu.make_async_remote_copy(
            src_ref=part,
            dst_ref=away,
            send_sem=s.fs.at[slot, k],
            recv_sem=s.fr.at[slot, idx],
            device_id=(b, a + 1 - 2 * core),
            device_id_type=MESH,
        )

    def each(first, body):
        if CHIPS <= 16:
            for k in range(first, CHIPS):
                body(k, 0)
        else:
            lax.fori_loop(first, CHIPS, body, 0)

    def gather_send(slot, ref, rows):
        def body(k, carry):
            gather_copy(slot, k, ref, rows).start()
            return carry

        each(1, body)
        forward(slot, 0, ref, rows, True).start()

    def gather_recv(slot, ref, rows):
        def relay(k, carry):
            idx, target = other(k)
            pltpu.make_async_remote_copy(
                src_ref=ref.at[a, b, rows],
                dst_ref=ref.at[target[1], target[0], rows],
                send_sem=s.gs.at[place_of(slot), k],
                recv_sem=s.gr.at[place_of(slot), idx],
                device_id=target,
                device_id_type=MESH,
            ).wait_recv()
            forward(slot, k, ref, rows, True).start()
            return carry

        each(1, relay)

        def collect(k, carry):
            forward(slot, k, ref, rows, False).wait_recv()
            return carry

        each(0, collect)

    def gather_done(slot, ref, rows):
        def body(k, carry):
            gather_copy(slot, k, ref, rows).wait_send()
            return carry

        lax.fori_loop(1, CHIPS, body, 0)

        def sent(k, carry):
            forward(slot, k, ref, rows, True).wait_send()
            return carry

        lax.fori_loop(0, CHIPS, sent, 0)

    def edges_of_guess(i, carry):
        s.gs_col[0, pl.ds(i, 1), :] = guess_ref[i, 0:1, :]
        s.gs_col[1, pl.ds(i, 1), :] = guess_ref[i, CS - 1 : CS, :]
        return carry

    lax.fori_loop(0, CS, edges_of_guess, 0)
    classes = map_ref[...]
    conduct = jnp.zeros(classes.shape, F32)
    for k in range(class_ref.shape[0]):
        conduct = jnp.where(classes == k, class_ref[k], conduct)
    s.field[...] = jnp.zeros(s.field.shape, F32)
    s.field[0:CS, 0:CS] = conduct
    s.cfield[...] = jnp.transpose(s.field[...])[0:ES]
    run = MODES * W
    for i in range(MODES * N):
        line, left = divmod(i * run, COLS)
        s.k0[a, b, line : line + 1, left : left + run] = coarse_ref[i : i + 1]

    guess_sends = exchange(
        0, lambda i: guess_ref.at[i * (CS - 1)], lambda i: s.gs_col.at[i], None
    )
    tile = lambda i: s.cfield.at[pl.ds(i * (ES - SUB), SUB)]
    cond_sends = exchange(1, lambda i: s.cfield, tile, lambda i: tile(i % 2))
    pl.semaphore_wait(barrier, count)
    send(cond_sends)
    send(guess_sends)
    k_rows = pl.ds(0, KR)
    gather_send(0, s.k0, k_rows)

    step = 256
    numbering = wrow_ref[...]
    tall_numbering = jnp.transpose(jnp.broadcast_to(numbering, (LANES, LOCAL)))
    lane = lax.broadcasted_iota(jnp.int32, (LOCAL, LANES), 1)
    for c in range(0, LOCAL, LANES):
        s.perm_t[:, c : c + LANES] = jnp.where(lane + c == tall_numbering, 1.0, 0.0).astype(BF16)

    NE = 2 * H * ES
    line = lax.broadcasted_iota(jnp.int32, (NE, LOCAL), 0)
    col = line >> int(math.log2(ES))
    col = jnp.where(col < H, col + lo, col - H + hi)
    pos = (line & (ES - 1)) * ES + col
    s.perm[0:NE, :] = jnp.where(pos == numbering, 1.0, 0.0).astype(BF16)

    def hot(i, carry):
        off = pl.multiple_of(i * step, step)
        pos = lax.broadcasted_iota(jnp.int32, (step, LOCAL), 0) + off
        s.perm[pl.ds(NE + off, step), :] = jnp.where(pos == numbering, 1.0, 0.0).astype(BF16)
        return carry

    lax.fori_loop(0, LOCAL // step, hot, 0)
    basis = basis_ref[0, 0]
    place = lax.rem(b, 3) * (MODES * N) + a * MODES
    line = lax.broadcasted_iota(jnp.int32, (LANES, LOCAL), 0) - place
    s.spread[...] = jnp.zeros(s.spread.shape, F32)
    for m in range(MODES):
        s.spread[...] = jnp.where(line == m, basis[m : m + 1], s.spread[...])
    b_high, b_low = split(jnp.transpose(s.spread[...]))
    both = dot(s.perm[NE:, :], jnp.concatenate([b_high, b_low], axis=1))
    s.aux[...] = both[:, 0:LANES] + both[:, LANES:]
    for k, first in enumerate((lo, hi)):
        for j in range(H):
            s.as_col[k, j] = s.aux[pl.ds(first + j, ES, stride=ES), :]
    aux_sends = exchange(
        2,
        lambda i: s.aux.at[pl.ds((lo, hi)[i] * ES, H * ES)],
        lambda i: s.as_col.at[i],
        lambda i: s.as_col.at[i % 2, pl.ds(0, H), pl.ds((ES - SUB) * (i // 2), SUB)],
    )

    def place_guess(i, carry):
        for h in range(HV):
            s.gd[h, pl.ds(at(OV + i, OV), CS), :] = guess_ref[i, :, half(h)]
            s.sol[h, i, 0:CS, :] = guess_ref[i, :, half(h)]
        return carry

    lax.fori_loop(0, CS, place_guess, 0)
    recv(guess_sends)
    recv(cond_sends)
    for h in range(HV):
        for side in range(2):
            edge = OV - 1 + side * (CS + 1)
            s.gd[h, pl.ds(at(edge, OV), CS), :] = s.g_row[side, :, half(h)]
            s.gd[h, pl.ds(at(OV, edge), CS, stride=DW), :] = s.g_col[side, :, half(h)]
    stack = (
        (s.c_cor.at[0], s.c_row.at[0], s.c_cor.at[1]),
        (s.c_col.at[0], s.cfield, s.c_col.at[1]),
        (s.c_cor.at[2], s.c_row.at[1], s.c_cor.at[3]),
    )
    for k, (left, mid, right) in enumerate(stack):
        s.cst[k, 0:H] = left[CS - H - (ES - SUB) : CS - (ES - SUB)]
        s.cst[k, H : H + CS] = mid[0:CS]
        s.cst[k, H + CS : DW] = right[0:H]
    clane = lax.broadcasted_iota(jnp.int32, s.cst.shape[1:], 1)
    cmap = jnp.where(
        clane < H,
        pltpu.roll(s.cst[0], LANES - (CS - H), 1),
        jnp.where(
            clane < H + CS, pltpu.roll(s.cst[1], H, 1), pltpu.roll(s.cst[2], H + CS, 1)
        ),
    )
    for r in range(DW):
        s.cond[pl.ds(r * DW, DW), :] = jnp.broadcast_to(cmap[0:DW, r : r + 1], (DW, LANES))
    col_pos = b * CS - OV + lax.broadcasted_iota(jnp.int32, (ES, LANES), 0)
    col_in = jnp.where((col_pos >= 0) & (col_pos < CS * W), 1.0, 0.0)

    def faces(u, carry):
        row_pos = a * CS - OV + u
        inside = jnp.where((row_pos >= 0) & (row_pos < CS * N), col_in, 0.0)
        cond = lambda du, dt: s.cond[pl.ds(at(u + du, dt), ES), :]
        own = cond(0, 0)
        halved = 0.5 * inside
        parts = [halved * (own + cond(*o)) for o in ((-1, 0), (1, 0), (0, -1), (0, 1))]
        here = pl.ds(pl.multiple_of(u * ES, ES), ES)
        s.wt[0, here, :] = REACTION * inside + ((parts[0] + parts[1]) + (parts[2] + parts[3]))
        for k in range(4):
            s.wt[1 + k, here, :] = parts[k]
        return carry

    lax.fori_loop(0, ES, faces, 0)

    def operator(read, u, t, n):
        weights = [s.wt[k, pl.ds(u * ES + t, n), :] for k in range(5)]
        out = []
        for h in range(HV):
            v = lambda du, dt: read(h, pl.ds(at(u + du, t + dt), n))
            around = weights[1] * v(-1, 0) + weights[2] * v(1, 0)
            beside = weights[3] * v(0, -1) + weights[4] * v(0, 1)
            out.append(weights[0] * v(0, 0) - (around + beside))
        return out

    def own_residual(i, carry):
        u = OV + i
        image = operator(lambda h, rows: s.gd[h, rows, :], u, OV, CS)
        for h in range(HV):
            s.res[h, pl.ds(u * ES + OV, CS), :] = rhs_ref[i, :, half(h)] - image[h]
        return carry

    lax.fori_loop(0, CS, own_residual, 0)

    near = (OV, CS)
    for k in range(2):
        for h in range(HV):
            for q in range(OV):
                s.rs_col[k, h, q] = s.res[h, pl.ds(near[k] + q, ES, stride=ES), :]
            s.rs_row[k, h] = s.res[h, near[k] * ES : (near[k] + OV) * ES, :]
    for k in range(4):
        for h in range(HV):
            for r in range(OV):
                cell = (near[k // 2] + r) * ES + near[k % 2]
                s.rs_cor[k, h, r * OV : (r + 1) * OV, :] = s.res[h, cell : cell + OV, :]
    res_sends = exchange(
        3,
        lambda i: s.rs_row.at[i],
        lambda i: s.rs_col.at[i],
        lambda i: s.rs_cor.at[i],
    )
    send(res_sends)
    send(aux_sends)

    load.wait()

    def right_side_perm(i, carry):
        tall = 2 * step
        rows = pl.ds(pl.multiple_of(i * tall, tall), tall)
        high, low = split(s.inv[rows, :])
        both = dot(jnp.concatenate([high, low], axis=0), s.perm_t[...]).astype(BF16)
        s.t_high[rows, :] = both[0:tall]
        s.t_low[rows, :] = both[tall:]
        return carry

    lax.fori_loop(0, LOCAL // (2 * step), right_side_perm, 0)
    m_high, m_low = split(jnp.concatenate([basis, jnp.zeros((SUB - MODES, LOCAL), F32)], axis=0))
    s.bw[...] = dot(jnp.concatenate([m_high, m_low], axis=0), s.perm_t[...]).astype(BF16)

    def set_x(u, value):
        high, low = split(jnp.concatenate(value, axis=1))
        rows = pl.ds(pl.multiple_of(u * ES, ES), ES)
        s.x_high[rows, :] = high
        s.x_low[rows, :] = low

    recv(res_sends)
    far = (0, OV + CS)
    for h in range(HV):
        for k in range(2):
            for q in range(OV):
                line = slice(q * ES + OV, q * ES + OV + CS)
                s.res[h, pl.ds((far[k] + q) * ES + OV, CS), :] = s.r_row[k, h, line, :]
                line = pl.ds(OV * ES + far[k] + q, CS, stride=ES)
                s.res[h, line, :] = s.r_col[k, h, q, OV : OV + CS, :]
        for k in range(4):
            for r in range(OV):
                cell = (far[k // 2] + r) * ES + far[k % 2]
                s.res[h, cell : cell + OV, :] = s.r_cor[k, h, r * OV : (r + 1) * OV, :]

    def first_x(u, carry):
        set_x(u, [s.res[h, pl.ds(u * ES, ES), :] for h in range(HV)])
        return carry

    lax.fori_loop(0, ES, first_x, 0)

    def coarse_rows():
        both = dot(s.bw[...], s.x_high[...])
        return both[0:SUB] + (both[SUB:] + dot(s.bw[0:SUB, :], s.x_low[...]))

    def left_side_perm(i, carry):
        big = (NE + LOCAL) // 2
        rows = pl.ds(pl.multiple_of(i * big, big), big)
        s.l_high[rows, :] = dot(s.perm[rows, :], s.t_high[...]).astype(BF16)
        s.l_low[rows, :] = dot(s.perm[rows, :], s.t_low[...]).astype(BF16)
        return carry

    def build_phi():
        recv(aux_sends)
        for i in range(CS):
            s.daux[pl.ds(at(OV + i, OV), CS), :] = s.aux[pl.ds((OV + i) * ES + OV, CS), :]
        for k in range(2):
            for j in range(H):
                deep_line = k * (CS + H) + j
                s.daux[pl.ds(deep_line * DW + H, CS), :] = s.a_row[
                    k, j * ES + OV : j * ES + OV + CS, :
                ]
                s.daux[pl.ds(H * DW + deep_line, CS, stride=DW), :] = s.a_col[
                    k, j, OV : OV + CS, :
                ]
        for k in range(4):
            first = lo if k // 2 else base
            for q in range(H):
                cell = (k // 2) * (CS + H) * DW + (k % 2) * (CS + H) + q
                for r in range(H):
                    s.daux[pl.ds(cell + r * DW, 1), :] = s.a_cor[k, q, first + r : first + r + 1, :]
        chunk = RP // 2

        def body(i, carry):
            rows = pl.ds(pl.multiple_of(i * chunk, chunk), chunk)
            value = s.daux[rows, :]
            high = value.astype(BF16).astype(F32)
            low = value - high
            if 2 * LK <= LANES:
                s.phi[rows, 0:LANES] = (high + pltpu.roll(low, LK, 1)).astype(BF16)
                s.phi[rows, LANES:] = high.astype(BF16)
            else:
                s.phi[rows, 0:LANES] = high.astype(BF16)
                s.phi[rows, LANES : 2 * LANES] = low.astype(BF16)
                s.phi[rows, 2 * LANES :] = high.astype(BF16)
            return carry

        lax.fori_loop(0, 2, body, 0)

    def build_kmat():
        gather_recv(0, s.k0, k_rows)
        per = COLS // (4 * W)
        wide_cols = MODES * W
        group = MODES * N
        piece = lax.broadcasted_iota(jnp.int32, (group, COLS), 0) & (per - 1)
        lane = lax.broadcasted_iota(jnp.int32, (group, COLS), 1)
        keep = (lane >> int(math.log2(wide_cols))) == piece
        width = N * W * SUB
        j = lax.broadcasted_iota(jnp.int32, (COLS, width), 0) & (wide_cols - 1)
        c = lax.broadcasted_iota(jnp.int32, (COLS, width), 1)
        total_high = total_low = None
        for a2 in range(N):
            blocks = []
            for third in range(3):
                db = lax.rem(third - b + 1 + 3 * W, 3) - 1
                spot = jnp.clip(b + db, 0, W - 1)
                raw = s.k0[a2, spot, 0:KR, :]
                tall = jnp.concatenate(
                    [jnp.broadcast_to(raw[r : r + 1], (per, COLS)) for r in range(KR)], axis=0
                )
                blocks.append(jnp.where(keep, tall, 0.0))
            if 2 * LK <= LANES:
                blocks = blocks * 2
            fill = LANES - len(blocks) * group
            blocks.append(jnp.zeros((fill, COLS), F32))
            high, low = split(jnp.concatenate(blocks, axis=0))
            fold = c == a2 * (W * SUB) + (j >> 2) * SUB + (j & 3)
            fold = jnp.where(fold, 1.0, 0.0).astype(BF16)
            th, tl = dot(high, fold), dot(low, fold)
            total_high = th if total_high is None else total_high + th
            total_low = tl if total_low is None else total_low + tl
        s.kmat[0] = total_high.astype(BF16)
        s.kmat[1] = total_low.astype(BF16)

    sub_pos = lax.broadcasted_iota(jnp.int32, (SUB, COLS), 0)
    pending = [guess_sends, cond_sends, aux_sends, res_sends]
    numer = denom = None
    sizes = []
    spans = []
    for it in range(ITERS + 1):
        ref = s.g.at[it]
        first = MODES if it == ITERS else 0
        last = MODES if it == 0 else MODES + 2
        span = pl.ds(first, last - first)
        spans.append(span)
        rows = coarse_rows() if it < ITERS else jnp.zeros((SUB, COLS), F32)
        if it > 0:
            rows = jnp.where(sub_pos == MODES, numer, rows)
            rows = jnp.where(sub_pos == MODES + 1, denom, rows)
        ref[a, b] = rows
        gather_send(it + 1, ref, span)
        if it < ITERS:
            if it == 0:
                left_side_perm(0, 0)
            high = s.l_high[0:NE, :]
            both = dot(jnp.concatenate([high, s.l_low[0:NE, :]], axis=0), s.x_high[...])
            value = both[0:NE] + (both[NE:] + dot(high, s.x_low[...]))
            for k in range(2):
                for j in range(H):
                    line = (k * H + j) * ES
                    for h in range(HV):
                        s.zs_col[it, k, h, j] = value[line : line + ES, half(h)]
            for k in range(4):
                u0 = hi if k // 2 else lo
                skip = ((H - 1) * (k // 2), (H - 1) * (k % 2))
                n = 0
                for r in range(H):
                    for j in range(H):
                        if (r, j) == ((H - 1) - skip[0], (H - 1) - skip[1]):
                            continue
                        for h in range(HV):
                            s.zs_cor[it, k, h, n : n + 1, :] = s.zs_col[
                                it, k % 2, h, j, u0 + r : u0 + r + 1, :
                            ]
                        n += 1
            copies = exchange(
                4 + it,
                lambda i: s.zs_row.at[it, i],
                lambda i: s.zs_col.at[it, i],
                lambda i: s.zs_cor.at[it, i],
            )
            send(copies, SIDES)
            if it == 0:
                left_side_perm(1, 0)

            def solve(i, carry):
                rows = pl.ds(NE + pl.multiple_of(i * step, step), step)
                high = s.l_high[rows, :]
                both = dot(jnp.concatenate([high, s.l_low[rows, :]], axis=0), s.x_high[...])
                value = both[0:step] + (both[step:] + dot(high, s.x_low[...]))
                for j in range(step // ES):
                    u = i * (step // ES) + j
                    for h in range(HV):
                        s.wdeep[h, pl.ds(at(u, 0), ES), :] = value[j * ES : (j + 1) * ES, half(h)]
                return carry

            lax.fori_loop(0, LOCAL // step, solve, 0)
            for k, u in enumerate((lo, hi)):
                for h in range(HV):
                    for r in range(H):
                        s.zs_row[it, k, h, r] = s.wdeep[h, pl.ds(at(u + r, 0), ES), :]
            send(copies, ENDS)
            pending.append(copies)
        if it == 0:
            build_phi()
            build_kmat()
            for early in pending[0:4]:
                done(early)
            gather_done(0, s.k0, k_rows)
        else:
            done(pending[3 + it])
            gather_done(it, s.g.at[it - 1], spans[it - 1])
        if it >= 2:
            old = sizes[it - 2]

            def advance(i, carry):
                for h in range(HV):
                    here = s.deep[it % 2, h, pl.ds(at(OV + i, OV), CS), :]
                    s.sol[h, i, 0:CS, :] = s.sol[h, i, 0:CS, :] + old[:, half(h)] * here
                return carry

            lax.fori_loop(0, CS, advance, 0)
        gather_recv(it + 1, ref, span)
        everyone = ref[...].reshape(N * W, SUB, COLS)
        if it > 0:
            total = jnp.sum(everyone, axis=0)
            size = total[MODES : MODES + 1] / total[MODES + 1 : MODES + 2]
            sizes.append(size)
        if it == ITERS:
            break
        coarse_only = lax.broadcasted_iota(jnp.int32, everyone.shape, 1) < MODES
        everyone = jnp.where(coarse_only, everyone, 0.0)
        g_high, g_low = split(everyone.reshape(N * W * SUB, COLS))
        s_high, s_low = split(dot3(s.kmat[0], s.kmat[1], g_high, g_low))
        if 2 * LK <= LANES:
            s_all = jnp.concatenate([s_high, s_low], axis=0)
        else:
            s_all = jnp.concatenate([s_high, s_high, s_low], axis=0)
        recv(copies)
        for h in range(HV):
            for k in range(2):
                for j in range(H):
                    deep_line = k * (CS + H) + j
                    s.wdeep[h, pl.ds(deep_line * DW + H, CS), :] = s.z_row[
                        it, k, h, j, OV : OV + CS, :
                    ]
                    s.wdeep[h, pl.ds(H * DW + deep_line, CS, stride=DW), :] = s.z_col[
                        it, k, h, j, OV : OV + CS, :
                    ]
            for k in range(4):
                skip = ((H - 1) * (k // 2), (H - 1) * (k % 2))
                n = 0
                for r in range(H):
                    for j in range(H):
                        if (r, j) == skip:
                            continue
                        cell = ((k // 2) * (CS + H) + r) * DW + (k % 2) * (CS + H) + j
                        s.wdeep[h, pl.ds(cell, 1), :] = s.z_cor[it, k, h, n : n + 1, :]
                        n += 1
        chunk = RP // 2
        now, before = it % 2, 1 - it % 2

        def coarse_part(i, carry):
            rows = pl.ds(pl.multiple_of(i * chunk, chunk), chunk)
            value = dot(s.phi[rows, :], s_all)
            for h in range(HV):
                part = value[:, half(h)] + s.wdeep[h, rows, :]
                if it > 0:
                    part = s.deep[before, h, rows, :] - size[:, half(h)] * part
                s.deep[now, h, rows, :] = part
            return carry

        lax.fori_loop(0, 2, coarse_part, 0)
        read = lambda h, rows: s.deep[now, h, rows, :]
        if it < ITERS - 1:

            def margin(q, carry):
                u = jnp.where(q < OV, q, q + CS)
                set_x(u, operator(read, u, 0, ES))
                return carry

            lax.fori_loop(0, 2 * OV, margin, 0)

        def apply(i, carry):
            u = OV + i
            value = operator(read, u, 0, ES)
            if it < ITERS - 1:
                set_x(u, value)
            line = pl.ds(pl.multiple_of(u * ES, ES), ES)
            sums = []
            for h in range(HV):
                left = s.res[h, line, :]
                if it > 0:
                    left = left - size[:, half(h)] * s.img[h, i]
                    s.res[h, line, :] = left
                s.img[h, i] = value[h]
                sums.append(carry[2 * h] + left * value[h])
                sums.append(carry[2 * h + 1] + value[h] * value[h])
            return tuple(sums)

        nothing = jnp.zeros((ES, LANES), F32)
        sums = lax.fori_loop(0, CS, apply, (nothing,) * (2 * HV))
        col = lax.broadcasted_iota(jnp.int32, (ES, LANES), 0)
        mine = (col >= OV) & (col < OV + CS)
        sums = [jnp.sum(jnp.where(mine, v, 0.0), axis=0, keepdims=True) for v in sums]
        numer = jnp.concatenate(sums[0::2], axis=1)
        denom = jnp.concatenate(sums[1::2], axis=1)

    size = sizes[-1]

    def finish(i, carry):
        u = OV + i
        for h in range(HV):
            step_of = size[:, half(h)]
            here = s.deep[(ITERS - 1) % 2, h, pl.ds(at(u, OV), CS), :]
            sol_out[i, :, half(h)] = s.sol[h, i, 0:CS, :] + step_of * here
            here = s.img[h, i, OV : OV + CS, :]
            res_out[i, :, half(h)] = s.res[h, pl.ds(u * ES + OV, CS), :] - step_of * here
        return carry

    lax.fori_loop(0, CS, finish, 0)
    gather_done(ITERS + 1, s.g.at[ITERS], spans[ITERS])


def local(
    N,
    W,
    right_side,
    initial_guess,
    class_map,
    class_conductivity,
    window_index,
    local_inverse,
    coarse_basis,
    coarse_inverse,
):
    CS, _, COLS = right_side.shape
    MODES, LOCAL = coarse_basis.shape[2:]
    ES = math.isqrt(LOCAL)
    OV = (ES - CS) // 2
    H = OV + 1
    DW = ES + 2
    RP = -(-DW * DW // 32) * 32
    HV = COLS // LANES
    KR = coarse_inverse.size // COLS
    K0 = -(-KR // SUB) * SUB
    CHIPS = N * W // 2
    PK = (2 if 6 * MODES * N <= LANES else 3) * LANES
    TALL = -(-DW // SUB) * SUB
    vmem = pl.BlockSpec(memory_space=pltpu.VMEM)
    scratch = dict(
        inv=((LOCAL, LOCAL), F32),
        perm=((2 * H * ES + LOCAL, LOCAL), BF16),
        perm_t=((LOCAL, LOCAL), BF16),
        t_high=((LOCAL, LOCAL), BF16),
        t_low=((LOCAL, LOCAL), BF16),
        l_high=((2 * H * ES + LOCAL, LOCAL), BF16),
        l_low=((2 * H * ES + LOCAL, LOCAL), BF16),
        bw=((2 * SUB, LOCAL), BF16),
        spread=((LANES, LOCAL), F32),
        x_high=((LOCAL, COLS), BF16),
        x_low=((LOCAL, COLS), BF16),
        field=((LANES, LANES), F32),
        cfield=((ES, LANES), F32),
        cst=((3, TALL, LANES), F32),
        cond=((RP, LANES), F32),
        wt=((5, LOCAL, LANES), F32),
        gd=((HV, RP, LANES), F32),
        sol=((HV, CS, ES, LANES), F32),
        res=((HV, LOCAL, LANES), F32),
        img=((HV, CS, ES, LANES), F32),
        aux=((LOCAL, LANES), F32),
        daux=((RP, LANES), F32),
        phi=((RP, PK), BF16),
        wdeep=((HV, RP, LANES), F32),
        deep=((2, HV, RP, LANES), F32),
        kmat=((2, LANES, N * W * SUB), BF16),
        k0=((N, W, K0, COLS), F32),
        g=((ITERS + 1, N, W, SUB, COLS), F32),
        gs_col=((2, CS, COLS), F32),
        g_row=((2, CS, COLS), F32),
        g_col=((2, CS, COLS), F32),
        c_row=((2, ES, LANES), F32),
        c_col=((2, SUB, LANES), F32),
        c_cor=((4, SUB, LANES), F32),
        as_col=((2, H, ES, LANES), F32),
        a_row=((2, H * ES, LANES), F32),
        a_col=((2, H, ES, LANES), F32),
        a_cor=((4, H, SUB, LANES), F32),
        rs_row=((2, HV, OV * ES, LANES), F32),
        rs_col=((2, HV, OV, ES, LANES), F32),
        rs_cor=((4, HV, SUB, LANES), F32),
        r_row=((2, HV, OV * ES, LANES), F32),
        r_col=((2, HV, OV, ES, LANES), F32),
        r_cor=((4, HV, SUB, LANES), F32),
        zs_row=((ITERS, 2, HV, H, ES, LANES), F32),
        zs_col=((ITERS, 2, HV, H, ES, LANES), F32),
        zs_cor=((ITERS, 4, HV, SUB, LANES), F32),
        z_row=((ITERS, 2, HV, H, ES, LANES), F32),
        z_col=((ITERS, 2, HV, H, ES, LANES), F32),
        z_cor=((ITERS, 4, HV, SUB, LANES), F32),
    )
    shapes = {name: pltpu.VMEM(*spec) for name, spec in scratch.items()}
    dma = pltpu.SemaphoreType.DMA
    shapes |= dict(
        ssem=dma((6, 8)),
        rsem=dma((6, 8)),
        gs=dma((3, CHIPS)),
        gr=dma((3, CHIPS)),
        fs=dma((3, CHIPS)),
        fr=dma((3, CHIPS)),
        lsem=dma,
    )
    anywhere = pl.BlockSpec(memory_space=pl.ANY)
    smem = pl.BlockSpec(memory_space=pltpu.SMEM)
    fields = pl.pallas_call(
        functools.partial(kernel, (N, W, ES, OV, CS, COLS, MODES, KR), tuple(shapes)),
        out_shape=(pltpu.VMEM(right_side.shape, F32),) * 2,
        in_specs=[vmem] * 3 + [smem, vmem, anywhere] + [vmem] * 2,
        out_specs=(vmem, vmem),
        scratch_shapes=list(shapes.values()),
        compiler_params=pltpu.CompilerParams(
            collective_id=0, has_side_effects=True, vmem_limit_bytes=60 * 1024 * 1024
        ),
        name="schwarz",
    )(
        right_side,
        initial_guess,
        class_map,
        class_conductivity,
        window_index[0],
        local_inverse[0, 0],
        coarse_basis,
        coarse_inverse,
    )
    return tuple(fields)


def solution(mesh):
    in_specs = (
        P("narrow", "wide", None),
        P("narrow", "wide", None),
        P("narrow", "wide"),
        P(),
        P("narrow", "wide", None),
        P("narrow", "wide", None, None),
        P("narrow", "wide", None, None),
        P("wide", "narrow"),
    )
    out_specs = (P("narrow", "wide", None), P("narrow", "wide", None))
    body = functools.partial(local, mesh.shape["narrow"], mesh.shape["wide"])
    return jax.shard_map(body, mesh=mesh, in_specs=in_specs, out_specs=out_specs, check_vma=False)
```
